256 devices in a mesh: dp: 4 (over y), seq: 8 (over x, core), tensor: 8 (over z).
Axes of the slice: x: 4, y: 4, z: 8, core: 2. Of those that a mesh axis runs over, the one named last changes fastest.
Arguments:
- tokens: bfloat16 [4, 4096, 8192], P('dp', ('seq', 'tensor')), may hold values from -19 to 19
- norm_gain: float32 [8192], replicated, may hold values from 0.1 to 1.9
- master_weight: float32 [8192, 3, 4096], P(('dp', 'seq'), None, 'tensor'), may hold values from -5 to 5
- short_filter: float32 [3, 3, 4096], P(None, None, 'tensor'), may hold values from -2600 to 2600
- medium_filter: bfloat16 [128, 4096], P(None, 'tensor'), may hold values from -1 to 1
- medium_skip: float32 [4096], P('tensor'), may hold values from 0.5 to 1.5
Outputs:
- mixed: bfloat16 [4, 4096, 4096], P('dp', 'seq', 'tensor')
- weight_amax: float32 [1], replicated
The draws below stay inside these ranges and needn't reach their ends.
All inputs are finite; a program needn't handle non-finite values.
Results may differ from the reference program's by a relative error of at most 0.015.
Values may be sent and summed in bfloat16 or wider, within the bound.
A program may use at most 128 MiB of HBM per device.

```python
import jax
import jax.numpy as jnp
from jax import lax

D = 8192
SHORT = 3
MED = 128
CH = 4096
SEQ_LEN = 4096
SEQS = 4


level_decades = 4.0


weight_base = 0.1


feature_level = 5.835e-05


def column_scales(key):
    scale_key = jax.random.fold_in(key, 71)
    spread_scale = jnp.exp(jax.random.uniform(scale_key, (1, 3, CH), jnp.float32, 0.0, jnp.log(10.0)))
    col_ramp = 1.5 ** (jnp.arange(CH, dtype=jnp.float32) / CH - 0.5)
    return spread_scale / 4.64 * col_ramp


def row_levels(key):
    ranking = jax.random.permutation(jax.random.fold_in(key, 53), D)
    jitter = jnp.exp(jax.random.uniform(jax.random.fold_in(key, 59), (D,), jnp.float32, 0.0, jnp.log(2.0)))
    position = (ranking.astype(jnp.float32) + 0.5) / D
    weight_level = jnp.exp(-level_decades * jnp.log(10.0) * position) * jitter
    token_level = jnp.exp(level_decades * jnp.log(10.0) * (position - 1.0)) / jitter
    peak_row = ranking == 0
    token_level = jnp.where(peak_row, 0.1 * token_level, token_level)
    return (weight_level, token_level, peak_row)


def draw_tokens(key, part):
    noise_key = jax.random.fold_in(key, 31)
    row_key = jax.random.fold_in(key, 37)
    noise = jax.random.truncated_normal(noise_key, -4.0, 4.0, (SEQS, SEQ_LEN, D), jnp.float32)
    row_scale = jnp.exp(jax.random.uniform(row_key, (SEQS, SEQ_LEN, 1), jnp.float32, 0.0, jnp.log(10.0))) / 4.64
    weight_level, token_level, peak_row = row_levels(key)
    return (noise * row_scale * token_level.reshape(1, 1, D)).astype(jnp.bfloat16)


def draw_master_weight(key, part):
    noise_key = jax.random.fold_in(key, 11)
    pick_key = jax.random.fold_in(key, 61)
    noise = jax.random.truncated_normal(noise_key, -4.0, 4.0, (D, 3, CH), jnp.float32)
    magnitude = jax.random.uniform(jax.random.fold_in(pick_key, 4), (), jnp.float32, 3.6, 4.9)
    weight_level, token_level, peak_row = row_levels(key)
    spread_part = noise * weight_base * weight_level.reshape(D, 1, 1) * column_scales(key)
    slot_index = jax.random.randint(jax.random.fold_in(pick_key, 1), (), 0, 3)
    channel_index = jax.random.randint(jax.random.fold_in(pick_key, 2), (), 0, CH)
    sign_bit = jax.random.randint(jax.random.fold_in(pick_key, 3), (), 0, 2)
    peak_entry = magnitude * (2 * sign_bit - 1).astype(jnp.float32)
    slot_hit = jnp.arange(3).reshape(1, 3, 1) == slot_index
    channel_hit = jnp.arange(CH).reshape(1, 1, CH) == channel_index
    entry_hit = peak_row.reshape(D, 1, 1) & slot_hit & channel_hit
    return jnp.where(entry_hit, peak_entry, spread_part)


def draw_short_filter(key, part):
    noise_key = jax.random.fold_in(key, 17)
    noise = jax.random.truncated_normal(noise_key, -4.0, 4.0, (3, SHORT, CH), jnp.float32)
    feature_scale = feature_level * jnp.sqrt(jnp.float32(D))
    return noise / jnp.sqrt(jnp.float32(SHORT)) / column_scales(key)[0][:, None, :] / feature_scale


def draw_medium_filter(key, part):
    noise_key = jax.random.fold_in(key, 19)
    rate_key = jax.random.fold_in(key, 23)
    lag_values = jnp.arange(MED, dtype=jnp.float32).reshape(MED, 1)
    noise = jax.random.truncated_normal(noise_key, -4.0, 4.0, (MED, CH), jnp.float32)
    rates = jnp.exp(jax.random.uniform(rate_key, (1, CH), jnp.float32, jnp.log(1.0 / 400.0), jnp.log(1.0 / 25.0)))
    return (noise * jnp.exp(-lag_values * rates) * 0.12).astype(jnp.bfloat16)


def levels(rng, extent, pieces, smallest, high):
    loudness = 1.0
    for dim, parts in pieces:
        draws = jax.random.uniform(jax.random.fold_in(jax.random.fold_in(rng, 6), dim), (parts,), jnp.float32, smallest / len(pieces), high / len(pieces))
        loudness = loudness * jnp.repeat(jnp.exp(draws), extent[dim] // parts).reshape((-1,) + (1,) * (len(extent) - 1 - dim))
    return loudness


def setup_inputs(seed: int = 0) -> dict:
    splits = jax.random.split(jax.random.key(seed), 7)
    tokens = draw_tokens(jax.random.fold_in(splits[6], 71), 0)
    norm_gain = jnp.clip(1.0 + 0.18 * jax.random.normal(splits[1], (D,), jnp.float32), 0.1, 1.9)
    master_weight = draw_master_weight(jax.random.fold_in(splits[6], 71), 0)
    short_filter = draw_short_filter(jax.random.fold_in(splits[6], 71), 0)
    medium_filter = draw_medium_filter(jax.random.fold_in(splits[6], 71), 0)
    medium_skip = jnp.clip(0.5 + 1.0 * jax.random.uniform(splits[5], (CH,), jnp.float32) ** levels(splits[5], (CH,), ((0, 8),), -0.2, 0.2), 0.5, 1.5)
    return dict(tokens=tokens, norm_gain=norm_gain, master_weight=master_weight, short_filter=short_filter, medium_filter=medium_filter, medium_skip=medium_skip)


power_steps = [2.0, 4.0, 16.0, 256.0, 65536.0, 4294967296.0, 1.8446744073709552e+19]

def exact_power(exponent):
    magnitude = jnp.abs(exponent)
    result = jnp.ones(exponent.shape, jnp.float32)
    for bit_place in range(7):
        chosen = magnitude >> bit_place & 1 == 1
        result = result * jnp.where(chosen, power_steps[bit_place], 1.0)
    return jnp.where(exponent >= 0, result, 1.0 / result)

def narrow_grid(entries):
    magnitude = jnp.abs(entries)
    exponent = jnp.floor(jnp.log2(jnp.maximum(magnitude, 1e-30))).astype(jnp.int32)
    quantum = exact_power(jnp.maximum(exponent, -6) - 3)
    return jnp.sign(entries) * jnp.floor(magnitude / quantum + 0.5) * quantum

def short_conv(padded, filters, length, margin):
    summed = jnp.zeros((length,) + padded.shape[1:], jnp.float32)
    for lag_index in range(filters.shape[1]):
        window = padded[margin - lag_index:margin - lag_index + length].astype(jnp.float32)
        summed = summed + filters[:, lag_index, :] * window
    return summed

def medium_conv(extended, filters, length):

    def add_tap(lag_index, summed):
        first_row = (filters.shape[0] - 1 - lag_index).astype(jnp.int32)
        window = lax.dynamic_slice_in_dim(extended, first_row, length, 0).astype(jnp.float32)
        tap_row = lax.dynamic_slice_in_dim(filters, lag_index.astype(jnp.int32), 1, 0).astype(jnp.float32)
        return summed + tap_row * window
    initial = jnp.zeros((length, filters.shape[1]), jnp.float32)
    return lax.fori_loop(0, filters.shape[0], add_tap, initial)

def reference(tokens, norm_gain, master_weight, short_filter, medium_filter, medium_skip):
    peak_value = jnp.max(jnp.abs(master_weight))
    factor = exact_power(jnp.floor(jnp.log2(448.0 / (peak_value + 1e-06))).astype(jnp.int32))
    recast = narrow_grid(master_weight * factor).astype(jnp.bfloat16).reshape(D, 3 * CH)

    def one_sequence(sequence):
        values = sequence.astype(jnp.float32)
        square_mean = lax.optimization_barrier(jnp.mean(values * values, axis=-1, keepdims=True))
        normed = (values * lax.rsqrt(square_mean + 1e-06) * norm_gain).astype(jnp.bfloat16)
        projected = jnp.dot(normed, recast, preferred_element_type=jnp.float32)
        features = (projected / factor).astype(jnp.bfloat16).reshape(SEQ_LEN, 3, CH)
        padded = jnp.concatenate([jnp.zeros((SHORT - 1, 3, CH), jnp.bfloat16), features], axis=0)
        mixed_conv = short_conv(padded, short_filter, SEQ_LEN, SHORT - 1)
        gated = (mixed_conv[:, 1] * mixed_conv[:, 2]).astype(jnp.bfloat16)
        extended = jnp.concatenate([jnp.zeros((MED - 1, CH), jnp.bfloat16), gated], axis=0)
        filtered = medium_conv(extended, medium_filter, SEQ_LEN) + medium_skip * gated.astype(jnp.float32)
        return (mixed_conv[:, 0] * filtered).astype(jnp.bfloat16)
    mixed_all = lax.map(one_sequence, tokens)
    return (mixed_all, peak_value.reshape(1))
```

```python
import functools
import heapq

import jax
import jax.numpy as jnp
import numpy as np
from jax import lax
from jax.experimental import pallas as pl
from jax.experimental.pallas import tpu as pltpu
from jax.sharding import PartitionSpec as P

MESH = pl.DeviceIdType.MESH
F32 = jnp.float32
BF16 = jnp.bfloat16
eps_norm = 1e-06
eps_peak = 1e-06
grid_top = 448.0

ring_slots = [0, 1, -1, 2, -2, 3, -3, 4]
slot_of = {d: s for s, d in enumerate(ring_slots)}
slot_of[-4] = slot_of[4]


def wrap4(d):
    return {-2: 2, 3: -1, -3: 1}.get(d, d)


def plan_messages():
    msgs = {}
    half_block = 32 * 8192 * 2
    for sign, link in ((1, "zp"), (-1, "zm")):
        for i in range(7):
            hop, sub = i // 2, i % 2
            if i == 6:
                sub = 0 if sign == 1 else 1
            dep = []
            if hop > 0:
                dep = [(link, i - 2 if i < 6 else (4 if sign == 1 else 5))]
            msgs[(link, i)] = (link, half_block, dep, ("tok", -sign * hop, sub))
    quarter = 64 * 1536 * 2

    def ring(half, axis, fixed, need):
        first = 2 * half
        for sign in (1, -1):
            link = axis + ("p" if sign == 1 else "m")
            order = (first, first + 1) if sign == 1 else (first + 1, first)
            names = [(half, link, fixed, n) for n in range(3)]
            place = lambda d: (0, d) if axis == "x" else (d, 0)
            spot = lambda d: (fixed, d) if axis == "x" else (d, fixed)
            for n in range(2):
                msgs[names[n]] = (link, quarter, need(order[n]), ("w",) + spot(0) + (order[n],))
            msgs[names[2]] = (link, quarter, [names[0]], ("w",) + spot(-sign) + (order[0],))

    def arrival(half, axis, fixed, d, q):
        first = 2 * half
        if d == 0:
            return []
        if d == 2:
            return [(half, axis + ("p" if q == first else "m"), fixed, 2)]
        sign = -d
        order = (first, first + 1) if sign == 1 else (first + 1, first)
        return [(half, axis + ("p" if sign == 1 else "m"), fixed, order.index(q))]

    ring(0, "x", 0, lambda q: [])
    ring(1, "y", 0, lambda q: [])
    got = {}
    for d in (0, -1, 1, 2):
        for q in (0, 1):
            got[(0, d, q)] = arrival(0, "x", 0, d, q)
        for q in (2, 3):
            got[(d, 0, q)] = arrival(1, "y", 0, d, q)
    second = {}
    for d in (0, -1, 1, 2):
        tag0, tag1 = ("s", d), ("s", d)

        def ring2(half, axis, across):
            first = 2 * half
            for sign in (1, -1):
                link = axis + ("p" if sign == 1 else "m")
                order = (first, first + 1) if sign == 1 else (first + 1, first)
                names = [(half, link, ("s", across), n) for n in range(3)]
                spot = lambda e: (across, e) if axis == "x" else (e, across)
                for n in range(2):
                    key = spot(0) + (order[n],)
                    msgs[names[n]] = (link, quarter, got[key], ("w",) + spot(0) + (order[n],))
                msgs[names[2]] = (link, quarter, [names[0]], ("w",) + spot(-sign) + (order[0],))
            for e in (-1, 1, 2):
                for q in (first, first + 1):
                    if e == 2:
                        name = (half, axis + ("p" if q == first else "m"), ("s", across), 2)
                    else:
                        sign = -e
                        order = (first, first + 1) if sign == 1 else (first + 1, first)
                        name = (half, axis + ("p" if sign == 1 else "m"), ("s", across), order.index(q))
                    second[spot(e) + (q,)] = [name]

        ring2(0, "y", d)
        ring2(1, "x", d)
    got.update(second)
    for dy in (0, -1, 1, 2):
        for dx in (0, -1, 1, 2):
            for h in (0, 1):
                need = got[(dy, dx, 2 * h)] + got[(dy, dx, 2 * h + 1)]
                msgs[("pair", dy, dx, h)] = ("core", 2 * quarter, need, ("half", dy, dx, h))
    return msgs, got


def timeline(msgs):
    rate = {"z": 46.0e3, "x": 46.0e3, "y": 46.0e3, "c": 250.0e3}
    children = {}
    for name, (_, _, need, _) in msgs.items():
        for dep in need:
            children.setdefault(dep, []).append(name)
    rank = {name: i for i, name in enumerate(msgs)}
    left = {name: len(need) for name, (_, _, need, _) in msgs.items()}
    ready = {}
    heap = []
    for name, (link, _, need, _) in msgs.items():
        if not need:
            ready[name] = 4.0 if link[0] == "z" else 15.0
            heapq.heappush(heap, (ready[name], rank[name], name))
    free, arrive, issue = {}, {}, {}
    while heap:
        at, _, name = heapq.heappop(heap)
        link, size, _, _ = msgs[name]
        start = max(at, free.get(link, 0.0))
        free[link] = start + size / rate[link[0]]
        issue[name] = at
        arrive[name] = free[link] + 1.5
        for child in children.get(name, ()):
            left[child] -= 1
            ready[child] = max(ready.get(child, 0.0), arrive[name])
            if left[child] == 0:
                heapq.heappush(heap, (ready[child], rank[child], child))
    return issue, arrive


def plan():
    msgs, got = plan_messages()
    issue, arrive = timeline(msgs)
    tok_need = {0: []}
    for sign, link in ((1, "zp"), (-1, "zm")):
        for hop in range(3):
            tok_need[-sign * (hop + 1)] = [(link, 2 * hop), (link, 2 * hop + 1)]
    tok_need[4] = [("zp", 6), ("zm", 6)]
    row_need = {}
    for dy in (0, -1, 1, 2):
        need = []
        for dx in (0, -1, 1, 2):
            for q in range(4):
                need += got[(dy, dx, q)]
            need += [("pair", dy, dx, h) for h in (0, 1)]
        row_need[dy] = need
    near = sum((tok_need[d] for d in (0, 1, -1, 2, -2)), [])
    mid = sum((tok_need[d] for d in (3, -3)), [])
    far = tok_need[4]
    tasks = [
        (near + row_need[0], 0, 320, 0),
        (near + row_need[-1], 0, 320, -1),
        (near + row_need[1], 0, 320, 1),
        (mid + row_need[0], 320, 448, 0),
        (mid + row_need[-1], 320, 448, -1),
        (mid + row_need[1], 320, 448, 1),
        (near + mid + row_need[2], 0, 448, 2),
        (far, 448, 512, None),
    ]
    events = [(issue[name], 0, i, ("send", name)) for i, name in enumerate(msgs)]
    for i, (need, lo, hi, dy) in enumerate(tasks):
        at = max(arrive[n] for n in need)
        if i and at < last:
            at = last
        last = at + 0.01
        events.append((at, 1, i, ("dot", need, lo, hi, dy)))
    events.sort(key=lambda e: e[:3])
    return msgs, [e[3] for e in events], max(arrive.values())


def dft_tables():
    n = np.arange(256)
    k = np.arange(128)[:, None]
    angle = 2.0 * np.pi * ((k * n[None, :]) % 256) / 256.0
    lower = np.sin(angle)
    lower[0] = np.cos(np.pi * n)
    full = np.concatenate([np.cos(angle), lower], axis=0)

    def split(a):
        a = a.astype(np.float32)
        hi = a.astype(BF16)
        lo = (a - hi.astype(np.float32)).astype(BF16)
        return np.stack([hi, lo])

    return split(full), split(full[:, 128:].T)


def round_grid(v):
    m = jnp.abs(v)
    t = m * F32(8388609.0)
    top = t - t * F32(1.0 - 2.0**-24)
    quantum = jnp.maximum(top, F32(2.0**-6)) * F32(0.125)
    magic = quantum * F32(1.5 * 2.0**23)
    r = (m + magic) - magic
    r = jnp.where(m - r == quantum * F32(0.5), r + quantum, r)
    return jnp.where(v < 0, -r, r)


def kernel(
    program,
    tok_hbm, gain_hbm, w_hbm, sf_hbm, mf_hbm, skip_hbm, f_hbm, g_hbm,
    out_ref, peak_ref,
    tok_in, gain, w_in, sf, mf, skip, fmat, gmat,
    a_all, w_all, acc, feat, gext, hspec, peaks,
    local_sem, send_sem, recv_sem, pk_send, pk_recv, halo_send, halo_recv,
):
    msgs, events, ids = program
    y = lax.axis_index("dp")
    s = lax.axis_index("seq")
    z = lax.axis_index("tensor")
    x, c = s // 2, s % 2

    ins = [(w_hbm, w_in), (tok_hbm, tok_in), (gain_hbm, gain), (mf_hbm, mf), (f_hbm, fmat), (g_hbm, gmat), (sf_hbm, sf), (skip_hbm, skip)]
    loads = [pltpu.make_async_copy(src, dst, local_sem.at[i]) for i, (src, dst) in enumerate(ins)]
    for load in loads:
        load.start()

    def dev(dy, ds, dz):
        return ((y + dy) % 4, ds, (z + dz) % 8)

    barrier = pltpu.get_barrier_semaphore()
    peers = [dev(0, s, k) for k in range(1, 8)] + [dev(0, (s + k) % 8, 0) for k in range(1, 8)] + [dev(k, s, 0) for k in range(1, 4)]
    for peer in peers:
        pl.semaphore_signal(barrier, inc=1, device_id=peer, device_id_type=MESH)

    loads[0].wait()
    top = jnp.zeros((8, 512), F32)
    part = [jnp.zeros((8, 512), F32) for _ in range(4)]
    for k in range(3):
        for r in range(0, 256, 32):
            for j in range(4):
                part[j] = jnp.maximum(part[j], jnp.abs(w_in[k, r + 8 * j : r + 8 * j + 8, :]))
    top = jnp.maximum(jnp.maximum(part[0], part[1]), jnp.maximum(part[2], part[3]))
    top = jnp.max(jnp.max(top, axis=0, keepdims=True), axis=1, keepdims=True)
    peaks[0] = jnp.broadcast_to(top, (8, 128))

    def norm_rows(lo):
        for r in range(lo, lo + 32, 16):
            v = tok_in[r : r + 16, :].astype(F32)
            mean = jnp.sum(v * v, axis=1, keepdims=True) * F32(1.0 / 8192)
            a_all[r : r + 16, :] = (v * lax.rsqrt(mean + F32(eps_norm)) * gain[...]).astype(BF16)

    loads[1].wait()
    loads[2].wait()
    norm_rows(0)

    def peak_round(src, base, targets):
        copies = []
        for i, target in enumerate(targets):
            copies.append(
                pltpu.make_async_remote_copy(
                    src_ref=peaks.at[src], dst_ref=peaks.at[3 + base + i],
                    send_sem=pk_send.at[base + i], recv_sem=pk_recv.at[base + i],
                    device_id=target, device_id_type=MESH,
                )
            )
        for copy in copies:
            copy.start()
        return copies

    def peak_finish(copies, src, base):
        best = peaks[src]
        for i, copy in enumerate(copies):
            copy.wait_recv()
            best = jnp.maximum(best, peaks[3 + base + i])
        return best

    def w_row(dy, dx, parity):
        return (((y + dy) % 4) * 8 + ((x + dx) % 4) * 2 + parity) * 256

    def message(name):
        link, _, _, place = msgs[name]
        if place[0] == "tok":
            _, d, sub = place
            step = 1 if link == "zp" else -1
            here = slot_of[d] * 64 + 32 * sub
            there = slot_of[d - step] * 64 + 32 * sub
            src, dst = a_all.at[here : here + 32, :], a_all.at[there : there + 32, :]
            target = dev(0, s, step)
        elif place[0] == "w":
            _, dy, dx, q = place
            row = pl.multiple_of(w_row(dy, dx, c) + 64 * q, 64)
            src = dst = w_all.at[pl.ds(row, 64), :]
            if link[0] == "x":
                target = dev(0, (s + (2 if link[1] == "p" else 6)) % 8, 0)
            else:
                target = dev(1 if link[1] == "p" else 3, s, 0)
        else:
            _, dy, dx, h = place
            row = pl.multiple_of(w_row(dy, dx, c) + 128 * h, 128)
            src = dst = w_all.at[pl.ds(row, 128), :]
            target = (y, x * 2 + 1 - c, z)
        i = ids[name]
        return pltpu.make_async_remote_copy(
            src_ref=src, dst_ref=dst, send_sem=send_sem.at[i], recv_sem=recv_sem.at[i], device_id=target, device_id_type=MESH
        )

    copies = {name: message(name) for name in msgs}
    arrived = set()

    def need(names):
        for name in names:
            if name not in arrived:
                arrived.add(name)
                copies[name].wait_recv()

    pl.semaphore_wait(barrier, len(peers))
    round0 = peak_round(0, 0, peers[:7])
    copies[("zp", 0)].start()
    copies[("zm", 0)].start()
    norm_rows(32)
    copies[("zp", 1)].start()
    copies[("zm", 1)].start()
    peaks[1] = peak_finish(round0, 0, 0)
    round1 = peak_round(1, 7, peers[7:14])
    peaks[2] = peak_finish(round1, 1, 7)
    round2 = peak_round(2, 14, peers[14:])
    peak = peak_finish(round2, 2, 14)
    peak_ref[0] = jnp.max(peak)

    ratio = F32(grid_top) / (peak + F32(eps_peak))
    factor = jnp.ones((8, 128), F32)
    inverse = jnp.ones((8, 128), F32)
    for p in (16, 8, 4, 2, 1):
        larger = factor * F32(2.0**p)
        over = ratio >= larger
        factor = jnp.where(over, larger, factor)
        inverse = jnp.where(over, inverse * F32(2.0**-p), inverse)
    factor = jnp.broadcast_to(factor[0:1, 0:1], (1, 512))
    inverse = jnp.broadcast_to(inverse[0:1, 0:1], (1, 512))
    own = pl.multiple_of(w_row(0, 0, c), 256)
    started = {("zp", 0), ("zm", 0), ("zp", 1), ("zm", 1)}

    def recast(i, carry):
        r = pl.multiple_of(i * 32, 32)
        for k in range(3):
            w_all[pl.ds(own + r, 32), 512 * k : 512 * k + 512] = round_grid(w_in[k, pl.ds(r, 32), :] * factor).astype(BF16)
        return carry

    lax.fori_loop(0, 8, recast, 0)

    def spectrum():
        for load in loads[3:]:
            load.wait()
        taps = mf[...]
        h = jnp.dot(fmat[0, :, 0:128], taps, preferred_element_type=F32) + jnp.dot(fmat[1, :, 0:128], taps, preferred_element_type=F32)
        first = lax.broadcasted_iota(jnp.int32, (128, 512), 0) == 0
        scale = jnp.where(first, F32(1.0 / 256), F32(2.0 / 256))
        hc, hs = h[0:128] * scale, h[128:256] * scale
        hspec[0] = hc
        hspec[1] = jnp.where(first, F32(0.0), hs)
        hspec[2] = jnp.where(first, hs, hc)

    def product(lo, hi, dy, fresh):
        rows = hi - lo
        if dy is None:
            k0, depth = 0, 8192
        else:
            k0, depth = pl.multiple_of(((y + dy) % 4) * 2048, 2048), 2048

        def column(i, carry):
            n = pl.multiple_of(i * 512, 512)
            left = a_all[lo:hi, :] if dy is None else a_all[lo:hi, pl.ds(k0, depth)]
            got = jnp.dot(left, w_all[pl.ds(k0, depth), pl.ds(n, 512)], preferred_element_type=F32)
            if fresh:
                acc[lo:hi, pl.ds(n, 512)] = got
            else:
                acc[lo:hi, pl.ds(n, 512)] += got
            return carry

        lax.fori_loop(0, 3, column, 0)

    touched = set()
    ready = False
    for event in events:
        if event[0] == "send":
            name = event[1]
            if name in started:
                continue
            need(msgs[name][2])
            copies[name].start()
            if not ready and msgs[name][2]:
                ready = True
                spectrum()
        else:
            _, names, lo, hi, dy = event
            need(names)
            product(lo, hi, dy, lo not in touched)
            touched.add(lo)
            if hi == 448 and lo == 0:
                touched.add(320)

    inverse_row = inverse
    for slot, d in enumerate(ring_slots):
        row = pl.multiple_of(8 + 64 * ((z + d) % 8), 8)
        for k in range(3):
            cols = slice(512 * k, 512 * k + 512)
            feat[pl.ds(row, 64), cols] = (acc[64 * slot : 64 * slot + 64, cols] * inverse_row).astype(BF16).astype(F32)

    after = (y, (s + 1) % 8, z)
    rim = pltpu.make_async_remote_copy(
        src_ref=feat.at[512:520, :], dst_ref=feat.at[0:8, :], send_sem=halo_send.at[0], recv_sem=halo_recv.at[0],
        device_id=after, device_id_type=MESH,
    )
    rim.start()

    def short(k, lo, rows):
        total = jnp.zeros((rows, 512), F32)
        for j in range(3):
            total = total + sf[k, j : j + 1, :] * feat[8 + lo - j : 8 + lo - j + rows, 512 * k : 512 * k + 512]
        return total

    def gate(lo, rows):
        gext[128 + lo : 128 + lo + rows, :] = (short(1, lo, rows) * short(2, lo, rows)).astype(BF16)

    gate(384, 128)
    edge = pltpu.make_async_remote_copy(
        src_ref=gext.at[512:640, :], dst_ref=gext.at[0:128, :], send_sem=halo_send.at[1], recv_sem=halo_recv.at[1],
        device_id=after, device_id_type=MESH,
    )
    edge.start()
    gate(256, 128)
    gate(128, 128)
    gate(16, 112)

    def mix(b):
        lo = 128 * b
        e = gext[lo : lo + 256, :]
        t = jnp.dot(fmat[0], e, preferred_element_type=F32) + jnp.dot(fmat[1], e, preferred_element_type=F32)
        tc, ts = t[0:128], t[128:256]
        pc = tc * hspec[0] - ts * hspec[1]
        ps = tc * hspec[1] + ts * hspec[2]
        p = jnp.concatenate([pc, ps], axis=0)
        ph = p.astype(BF16)
        pl_ = (p - ph.astype(F32)).astype(BF16)
        f = jnp.dot(gmat[0], ph, preferred_element_type=F32)
        f = f + jnp.dot(gmat[0], pl_, preferred_element_type=F32)
        f = f + jnp.dot(gmat[1], ph, preferred_element_type=F32)
        f = f + skip[...] * e[128:256].astype(F32)
        out_ref[lo : lo + 128, :] = (short(0, lo, 128) * f).astype(BF16)

    mix(3)
    mix(2)
    rim.wait_recv()
    edge.wait_recv()

    @pl.when(s == 0)
    def _():
        feat[0:8, :] = jnp.zeros((8, 1536), F32)
        gext[0:128, :] = jnp.zeros((128, 512), BF16)

    gate(0, 16)
    mix(1)
    mix(0)
    rim.wait_send()
    edge.wait_send()
    for copy in round0 + round1 + round2:
        copy.wait_send()
    for copy in copies.values():
        copy.wait_send()


def shards(tokens, norm_gain, master_weight, short_filter, medium_filter, medium_skip):
    msgs, events, _ = plan()
    ids = {name: i for i, name in enumerate(msgs)}
    ftab, gtab = dft_tables()
    count = len(msgs)
    any_space = pl.BlockSpec(memory_space=pl.ANY)
    mixed, peak = pl.pallas_call(
        functools.partial(kernel, (msgs, events, ids)),
        out_shape=(jax.ShapeDtypeStruct((512, 512), BF16), jax.ShapeDtypeStruct((1,), F32)),
        in_specs=[any_space] * 8,
        out_specs=(pl.BlockSpec(memory_space=pltpu.VMEM), pl.BlockSpec(memory_space=pltpu.SMEM)),
        scratch_shapes=[
            pltpu.VMEM((64, 8192), BF16),
            pltpu.VMEM((1, 8192), F32),
            pltpu.VMEM((3, 256, 512), F32),
            pltpu.VMEM((3, 3, 512), F32),
            pltpu.VMEM((128, 512), BF16),
            pltpu.VMEM((1, 512), F32),
            pltpu.VMEM((2, 256, 256), BF16),
            pltpu.VMEM((2, 128, 256), BF16),
            pltpu.VMEM((512, 8192), BF16),
            pltpu.VMEM((8192, 1536), BF16),
            pltpu.VMEM((512, 1536), F32),
            pltpu.VMEM((520, 1536), F32),
            pltpu.VMEM((640, 512), BF16),
            pltpu.VMEM((3, 128, 512), F32),
            pltpu.VMEM((20, 8, 128), F32),
            pltpu.SemaphoreType.DMA((8,)),
            pltpu.SemaphoreType.DMA((count,)),
            pltpu.SemaphoreType.DMA((count,)),
            pltpu.SemaphoreType.DMA((17,)),
            pltpu.SemaphoreType.DMA((17,)),
            pltpu.SemaphoreType.DMA((2,)),
            pltpu.SemaphoreType.DMA((2,)),
        ],
        compiler_params=pltpu.CompilerParams(collective_id=0, has_side_effects=True, vmem_limit_bytes=60 * 1024 * 1024),
    )(
        tokens.reshape(64, 8192),
        norm_gain.reshape(1, 8192),
        jnp.transpose(master_weight, (1, 0, 2)),
        short_filter,
        medium_filter,
        medium_skip.reshape(1, 512),
        jnp.asarray(ftab),
        jnp.asarray(gtab),
    )
    return mixed[None], peak


def solution(mesh):
    placed = (
        P("dp", ("seq", "tensor"), None),
        P(),
        P(("dp", "seq"), None, "tensor"),
        P(None, None, "tensor"),
        P(None, "tensor"),
        P("tensor"),
    )
    return jax.shard_map(
        shards,
        mesh=mesh,
        in_specs=placed,
        out_specs=(P("dp", "seq", "tensor"), P()),
        check_vma=False,
    )
```

```python
import functools
import heapq

import jax
import jax.numpy as jnp
import numpy as np
from jax import lax
from jax.experimental import pallas as pl
from jax.experimental.pallas import tpu as pltpu
from jax.sharding import PartitionSpec as P

MESH = pl.DeviceIdType.MESH
F32 = jnp.float32
BF16 = jnp.bfloat16
eps_norm = 1e-06
eps_peak = 1e-06
grid_top = 448.0

ring_slots = [0, 1, -1, 2, -2, 3, -3, 4]
slot_of = {d: s for s, d in enumerate(ring_slots)}
slot_of[-4] = slot_of[4]

chunks = [(0, None), (-1, None), (1, None), (2, 0), (2, -1), (2, 1), (2, 2)]


def wrap4(d):
    return {-2: 2, 3: -1, -3: 1}.get(d, d)


def plan_messages():
    msgs = {}
    for ci, (dy, dx) in enumerate(chunks):
        size = 64 * 2 * (2048 if dx is None else 512)
        for sign, link in ((1, "zp"), (-1, "zm")):
            for hop in range(4):
                dep = [(link, ci, hop - 1)] if hop else []
                sub = None if hop < 3 else (0 if sign == 1 else 1)
                msgs[(link, ci, hop)] = (link, size if hop < 3 else size // 2, dep, ("tok", -sign * hop, sub, ci))
    quarter = 64 * 1536 * 2

    def ring(half, axis, fixed, need):
        first = 2 * half
        for sign in (1, -1):
            link = axis + ("p" if sign == 1 else "m")
            order = (first, first + 1) if sign == 1 else (first + 1, first)
            names = [(half, link, fixed, n) for n in range(3)]
            place = lambda d: (0, d) if axis == "x" else (d, 0)
            spot = lambda d: (fixed, d) if axis == "x" else (d, fixed)
            for n in range(2):
                msgs[names[n]] = (link, quarter, need(order[n]), ("w",) + spot(0) + (order[n],))
            msgs[names[2]] = (link, quarter, [names[0]], ("w",) + spot(-sign) + (order[0],))

    def arrival(half, axis, fixed, d, q):
        first = 2 * half
        if d == 0:
            return []
        if d == 2:
            return [(half, axis + ("p" if q == first else "m"), fixed, 2)]
        sign = -d
        order = (first, first + 1) if sign == 1 else (first + 1, first)
        return [(half, axis + ("p" if sign == 1 else "m"), fixed, order.index(q))]

    ring(0, "x", 0, lambda q: [])
    ring(1, "y", 0, lambda q: [])
    got = {}
    for d in (0, -1, 1, 2):
        for q in (0, 1):
            got[(0, d, q)] = arrival(0, "x", 0, d, q)
        for q in (2, 3):
            got[(d, 0, q)] = arrival(1, "y", 0, d, q)
    second = {}
    for d in (0, -1, 1, 2):
        tag0, tag1 = ("s", d), ("s", d)

        def ring2(half, axis, across):
            first = 2 * half
            for sign in (1, -1):
                link = axis + ("p" if sign == 1 else "m")
                order = (first, first + 1) if sign == 1 else (first + 1, first)
                names = [(half, link, ("s", across), n) for n in range(3)]
                spot = lambda e: (across, e) if axis == "x" else (e, across)
                for n in range(2):
                    key = spot(0) + (order[n],)
                    msgs[names[n]] = (link, quarter, got[key], ("w",) + spot(0) + (order[n],))
                msgs[names[2]] = (link, quarter, [names[0]], ("w",) + spot(-sign) + (order[0],))
            for e in (-1, 1, 2):
                for q in (first, first + 1):
                    if e == 2:
                        name = (half, axis + ("p" if q == first else "m"), ("s", across), 2)
                    else:
                        sign = -e
                        order = (first, first + 1) if sign == 1 else (first + 1, first)
                        name = (half, axis + ("p" if sign == 1 else "m"), ("s", across), order.index(q))
                    second[spot(e) + (q,)] = [name]

        ring2(0, "y", d)
        ring2(1, "x", d)
    got.update(second)
    for dy in (0, -1, 1, 2):
        for dx in (0, -1, 1, 2):
            for h in (0, 1):
                need = got[(dy, dx, 2 * h)] + got[(dy, dx, 2 * h + 1)]
                msgs[("pair", dy, dx, h)] = ("core", 2 * quarter, need, ("half", dy, dx, h))
    return msgs, got


def urgency(name):
    if name[0] in ("zp", "zm"):
        _, ci, hop = name
        at = (0.0, 4.0, 8.0, 12.0, 13.0, 14.0, 15.0)[ci]
        return at + 2.0 * hop if hop or ci > 2 else ci - 10.0
    if name[0] == "pair":
        return 0.0
    half, _, across, n = name
    if not isinstance(across, tuple):
        return n * 0.1
    d = {0: 0, -1: 1, 1: 2, 2: 3}[across[1]]
    if half == 0:
        return 10.0 + d * 0.1 + (10.0 if n == 2 else 0.0)
    return 10.0 + 4.0 * d + n * 0.1


def timeline(msgs):
    rate = {"z": 46.0e3, "x": 46.0e3, "y": 46.0e3, "c": 250.0e3}
    children = {}
    for name, (_, _, need, _) in msgs.items():
        for dep in need:
            children.setdefault(dep, []).append(name)
    rank = {name: i for i, name in enumerate(msgs)}
    left = {name: len(need) for name, (_, _, need, _) in msgs.items()}
    ready = {name: 0.0 for name in msgs}
    queue = {link: [] for link in ("zp", "zm", "xp", "xm", "yp", "ym", "core")}
    heap = []
    for name, (link, _, need, _) in msgs.items():
        if not need:
            ready[name] = 5.0 if link[0] == "z" else 15.0
            heapq.heappush(heap, (ready[name], 0, rank[name], name))
    busy = set()
    arrive, issue = {}, {}

    def serve(link, now):
        if link in busy or not queue[link]:
            return
        _, _, name = heapq.heappop(queue[link])
        busy.add(link)
        done = now + msgs[name][1] / rate[link[0]]
        arrive[name] = done + 1.5
        issue[name] = now
        heapq.heappush(heap, (done, 1, rank[name], name))
        for child in children.get(name, ()):
            left[child] -= 1
            ready[child] = max(ready[child], arrive[name])
            if left[child] == 0:
                heapq.heappush(heap, (ready[child], 0, rank[child], child))

    while heap:
        now, kind, _, name = heapq.heappop(heap)
        link = msgs[name][0]
        if kind == 1:
            busy.discard(link)
        else:
            heapq.heappush(queue[link], (urgency(name), rank[name], name))
        if not heap or heap[0][0] > now:
            for key in queue:
                serve(key, now)
    lead = 3.0
    early = {name: max(ready[name], issue[name] - lead) for name in msgs}
    return early, arrive


def plan():
    msgs, got = plan_messages()
    issue, arrive = timeline(msgs)
    tok_need = {}
    for ci, (dy, dx) in enumerate(chunks):
        tok_need[(dy, dx)] = [(link, ci, hop) for link in ("zp", "zm") for hop in range(4)]
    tasks = []
    for dy in (0, -1, 1, 2):
        for dx in (0, -1, 1, 2):
            need = list(tok_need[(dy, None)] if (dy, None) in tok_need else tok_need[(dy, dx)])
            for q in range(4):
                need += got[(dy, dx, q)]
            need += [("pair", dy, dx, h) for h in (0, 1)]
            tasks.append((max(arrive[n] for n in need), need, dy, dx))
    tasks.sort(key=lambda t: t[0])
    events = [(issue[name], 0, i, ("send", name)) for i, name in enumerate(msgs)]
    at = 0.0
    for i, (when, need, dy, dx) in enumerate(tasks):
        at = max(at, when)
        events.append((at, 1, i, ("dot", need, dy, dx)))
        at += 1.3
    events.sort(key=lambda e: e[:3])
    placed, order = set(), []
    for event in events:
        if event[3][0] == "send":
            assert all(dep in placed for dep in msgs[event[3][1]][2])
            placed.add(event[3][1])
        order.append(event[3])
    return msgs, order, at


def dft_tables():
    n = np.arange(256)
    k = np.arange(128)[:, None]
    angle = 2.0 * np.pi * ((k * n[None, :]) % 256) / 256.0
    lower = np.sin(angle)
    lower[0] = np.cos(np.pi * n)
    full = np.concatenate([np.cos(angle), lower], axis=0)

    def split(a):
        a = a.astype(np.float32)
        hi = a.astype(BF16)
        lo = (a - hi.astype(np.float32)).astype(BF16)
        return np.stack([hi, lo])

    return split(full), split(full[:, 128:].T)


def round_grid(v):
    m = jnp.abs(v)
    t = m * F32(8388609.0)
    top = t - t * F32(1.0 - 2.0**-24)
    quantum = jnp.maximum(top, F32(2.0**-6)) * F32(0.125)
    magic = quantum * F32(1.5 * 2.0**23)
    r = (m + magic) - magic
    r = jnp.where(m - r == quantum * F32(0.5), r + quantum, r)
    return jnp.where(v < 0, -r, r)


def kernel(
    program,
    tok_hbm, gain_hbm, w_hbm, sf_hbm, mf_hbm, skip_hbm, f_hbm, g_hbm,
    out_ref, peak_ref,
    tok_in, gain, w_in, sf, mf, skip, fmat, gmat,
    a_all, w_all, acc, feat, gext, hspec, peaks,
    local_sem, send_sem, recv_sem, pk_send, pk_recv, halo_send, halo_recv,
):
    msgs, events, ids = program
    y = lax.axis_index("dp")
    s = lax.axis_index("seq")
    z = lax.axis_index("tensor")
    x, c = s // 2, s % 2

    ins = [(w_hbm, w_in), (tok_hbm, tok_in), (gain_hbm, gain), (mf_hbm, mf), (f_hbm, fmat), (g_hbm, gmat), (sf_hbm, sf), (skip_hbm, skip)]
    loads = [pltpu.make_async_copy(src, dst, local_sem.at[i]) for i, (src, dst) in enumerate(ins)]
    for load in loads:
        load.start()

    def dev(dy, ds, dz):
        return ((y + dy) % 4, ds, (z + dz) % 8)

    barrier = pltpu.get_barrier_semaphore()
    peers = [dev(0, s, k) for k in range(1, 8)] + [dev(0, (s + k) % 8, 0) for k in range(1, 8)] + [dev(k, s, 0) for k in range(1, 4)]
    for peer in peers:
        pl.semaphore_signal(barrier, inc=1, device_id=peer, device_id_type=MESH)

    loads[0].wait()
    top = jnp.zeros((8, 512), F32)
    part = [jnp.zeros((8, 512), F32) for _ in range(4)]
    for k in range(3):
        for r in range(0, 256, 32):
            for j in range(4):
                part[j] = jnp.maximum(part[j], jnp.abs(w_in[k, r + 8 * j : r + 8 * j + 8, :]))
    top = jnp.maximum(jnp.maximum(part[0], part[1]), jnp.maximum(part[2], part[3]))
    top = jnp.max(jnp.max(top, axis=0, keepdims=True), axis=1, keepdims=True)
    peaks[0] = jnp.broadcast_to(top, (8, 128))

    def norm_rows(lo):
        for r in range(lo, lo + 32, 16):
            v = tok_in[r : r + 16, :].astype(F32)
            mean = jnp.sum(v * v, axis=1, keepdims=True) * F32(1.0 / 8192)
            a_all[r : r + 16, :] = (v * lax.rsqrt(mean + F32(eps_norm)) * gain[...]).astype(BF16)

    loads[1].wait()
    loads[2].wait()
    norm_rows(0)
    norm_rows(32)

    def peak_round(src, base, targets):
        copies = []
        for i, target in enumerate(targets):
            copies.append(
                pltpu.make_async_remote_copy(
                    src_ref=peaks.at[src], dst_ref=peaks.at[3 + base + i],
                    send_sem=pk_send.at[base + i], recv_sem=pk_recv.at[base + i],
                    device_id=target, device_id_type=MESH,
                )
            )
        for copy in copies:
            copy.start()
        return copies

    def peak_finish(copies, src, base):
        best = peaks[src]
        for i, copy in enumerate(copies):
            copy.wait_recv()
            best = jnp.maximum(best, peaks[3 + base + i])
        return best

    def w_row(dy, dx, parity):
        return (((y + dy) % 4) * 8 + ((x + dx) % 4) * 2 + parity) * 256

    def message(name):
        link, _, _, place = msgs[name]
        if place[0] == "tok":
            _, d, sub, ci = place
            step = 1 if link == "zp" else -1
            off, rows = (0, 64) if sub is None else (32 * sub, 32)
            here = slot_of[d] * 64 + off
            there = slot_of[d - step] * 64 + off
            dy, dx = chunks[ci]
            if dx is None:
                cols = pl.ds(pl.multiple_of(((y + dy) % 4) * 2048, 2048), 2048)
            else:
                cols = pl.ds(pl.multiple_of(w_row(dy, dx, 0), 512), 512)
            src, dst = a_all.at[here : here + rows, cols], a_all.at[there : there + rows, cols]
            target = dev(0, s, step)
        elif place[0] == "w":
            _, dy, dx, q = place
            row = pl.multiple_of(w_row(dy, dx, c) + 64 * q, 64)
            src = dst = w_all.at[pl.ds(row, 64), :]
            if link[0] == "x":
                target = dev(0, (s + (2 if link[1] == "p" else 6)) % 8, 0)
            else:
                target = dev(1 if link[1] == "p" else 3, s, 0)
        else:
            _, dy, dx, h = place
            row = pl.multiple_of(w_row(dy, dx, c) + 128 * h, 128)
            src = dst = w_all.at[pl.ds(row, 128), :]
            target = (y, x * 2 + 1 - c, z)
        i = ids[name]
        return pltpu.make_async_remote_copy(
            src_ref=src, dst_ref=dst, send_sem=send_sem.at[i], recv_sem=recv_sem.at[i], device_id=target, device_id_type=MESH
        )

    copies = {name: message(name) for name in msgs}
    arrived = set()
    started = [(link, ci, 0) for ci in range(3) for link in ("zp", "zm")]

    def need(names):
        for name in names:
            if name not in arrived:
                arrived.add(name)
                copies[name].wait_recv()

    pl.semaphore_wait(barrier, len(peers))
    round0 = peak_round(0, 0, peers[:7])
    for name in started:
        copies[name].start()
    peaks[1] = peak_finish(round0, 0, 0)
    round1 = peak_round(1, 7, peers[7:14])
    peaks[2] = peak_finish(round1, 1, 7)
    round2 = peak_round(2, 14, peers[14:])
    peak = peak_finish(round2, 2, 14)
    peak_ref[0] = jnp.max(peak)

    ratio = F32(grid_top) / (peak + F32(eps_peak))
    factor = jnp.ones((8, 128), F32)
    inverse = jnp.ones((8, 128), F32)
    for p in (16, 8, 4, 2, 1):
        larger = factor * F32(2.0**p)
        over = ratio >= larger
        factor = jnp.where(over, larger, factor)
        inverse = jnp.where(over, inverse * F32(2.0**-p), inverse)
    factor = jnp.broadcast_to(factor[0:1, 0:1], (1, 512))
    inverse = jnp.broadcast_to(inverse[0:1, 0:1], (1, 512))
    own = pl.multiple_of(w_row(0, 0, c), 256)

    def recast(i, carry):
        r = pl.multiple_of(i * 32, 32)
        for k in range(3):
            w_all[pl.ds(own + r, 32), 512 * k : 512 * k + 512] = round_grid(w_in[k, pl.ds(r, 32), :] * factor).astype(BF16)
        return carry

    lax.fori_loop(0, 8, recast, 0)

    def spectrum():
        for load in loads[3:]:
            load.wait()
        taps = mf[...]
        h = jnp.dot(fmat[0, :, 0:128], taps, preferred_element_type=F32) + jnp.dot(fmat[1, :, 0:128], taps, preferred_element_type=F32)
        first = lax.broadcasted_iota(jnp.int32, (128, 512), 0) == 0
        scale = jnp.where(first, F32(1.0 / 256), F32(2.0 / 256))
        hc, hs = h[0:128] * scale, h[128:256] * scale
        hspec[0] = hc
        hspec[1] = jnp.where(first, F32(0.0), hs)
        hspec[2] = jnp.where(first, hs, hc)

    def product(dy, dx, fresh):
        k0 = pl.multiple_of(w_row(dy, dx, 0), 512)

        def column(i, carry):
            n = pl.multiple_of(i * 512, 512)
            got = jnp.dot(a_all[:, pl.ds(k0, 512)], w_all[pl.ds(k0, 512), pl.ds(n, 512)], preferred_element_type=F32)
            if fresh:
                acc[:, pl.ds(n, 512)] = got
            else:
                acc[:, pl.ds(n, 512)] += got
            return carry

        lax.fori_loop(0, 3, column, 0)

    fresh = True
    ready = False
    for event in events:
        if event[0] == "send":
            name = event[1]
            if name in started:
                continue
            need(msgs[name][2])
            copies[name].start()
            if not ready and msgs[name][2]:
                ready = True
                spectrum()
        else:
            _, names, dy, dx = event
            need(names)
            product(dy, dx, fresh)
            fresh = False

    inverse_row = inverse
    for slot, d in enumerate(ring_slots):
        row = pl.multiple_of(8 + 64 * ((z + d) % 8), 8)
        for k in range(3):
            cols = slice(512 * k, 512 * k + 512)
            feat[pl.ds(row, 64), cols] = (acc[64 * slot : 64 * slot + 64, cols] * inverse_row).astype(BF16).astype(F32)

    after = (y, (s + 1) % 8, z)
    rim = pltpu.make_async_remote_copy(
        src_ref=feat.at[512:520, :], dst_ref=feat.at[0:8, :], send_sem=halo_send.at[0], recv_sem=halo_recv.at[0],
        device_id=after, device_id_type=MESH,
    )
    rim.start()

    def short(k, lo, rows):
        total = jnp.zeros((rows, 512), F32)
        for j in range(3):
            total = total + sf[k, j : j + 1, :] * feat[8 + lo - j : 8 + lo - j + rows, 512 * k : 512 * k + 512]
        return total

    def gate(lo, rows):
        gext[128 + lo : 128 + lo + rows, :] = (short(1, lo, rows) * short(2, lo, rows)).astype(BF16)

    gate(384, 128)
    edge = pltpu.make_async_remote_copy(
        src_ref=gext.at[512:640, :], dst_ref=gext.at[0:128, :], send_sem=halo_send.at[1], recv_sem=halo_recv.at[1],
        device_id=after, device_id_type=MESH,
    )
    edge.start()
    gate(256, 128)
    gate(128, 128)
    gate(16, 112)

    def mix(b):
        lo = 128 * b
        e = gext[lo : lo + 256, :]
        t = jnp.dot(fmat[0], e, preferred_element_type=F32) + jnp.dot(fmat[1], e, preferred_element_type=F32)
        tc, ts = t[0:128], t[128:256]
        pc = tc * hspec[0] - ts * hspec[1]
        ps = tc * hspec[1] + ts * hspec[2]
        p = jnp.concatenate([pc, ps], axis=0)
        ph = p.astype(BF16)
        pl_ = (p - ph.astype(F32)).astype(BF16)
        f = jnp.dot(gmat[0], ph, preferred_element_type=F32)
        f = f + jnp.dot(gmat[0], pl_, preferred_element_type=F32)
        f = f + jnp.dot(gmat[1], ph, preferred_element_type=F32)
        f = f + skip[...] * e[128:256].astype(F32)
        out_ref[lo : lo + 128, :] = (short(0, lo, 128) * f).astype(BF16)

    mix(3)
    mix(2)
    rim.wait_recv()
    edge.wait_recv()

    @pl.when(s == 0)
    def _():
        feat[0:8, :] = jnp.zeros((8, 1536), F32)
        gext[0:128, :] = jnp.zeros((128, 512), BF16)

    gate(0, 16)
    mix(1)
    mix(0)
    rim.wait_send()
    edge.wait_send()
    for copy in round0 + round1 + round2:
        copy.wait_send()
    for copy in copies.values():
        copy.wait_send()


def shards(tokens, norm_gain, master_weight, short_filter, medium_filter, medium_skip):
    msgs, events, _ = plan()
    ids = {name: i for i, name in enumerate(msgs)}
    ftab, gtab = dft_tables()
    count = len(msgs)
    any_space = pl.BlockSpec(memory_space=pl.ANY)
    mixed, peak = pl.pallas_call(
        functools.partial(kernel, (msgs, events, ids)),
        out_shape=(jax.ShapeDtypeStruct((512, 512), BF16), jax.ShapeDtypeStruct((1,), F32)),
        in_specs=[any_space] * 8,
        out_specs=(pl.BlockSpec(memory_space=pltpu.VMEM), pl.BlockSpec(memory_space=pltpu.SMEM)),
        scratch_shapes=[
            pltpu.VMEM((64, 8192), BF16),
            pltpu.VMEM((1, 8192), F32),
            pltpu.VMEM((3, 256, 512), F32),
            pltpu.VMEM((3, 3, 512), F32),
            pltpu.VMEM((128, 512), BF16),
            pltpu.VMEM((1, 512), F32),
            pltpu.VMEM((2, 256, 256), BF16),
            pltpu.VMEM((2, 128, 256), BF16),
            pltpu.VMEM((512, 8192), BF16),
            pltpu.VMEM((8192, 1536), BF16),
            pltpu.VMEM((512, 1536), F32),
            pltpu.VMEM((520, 1536), F32),
            pltpu.VMEM((640, 512), BF16),
            pltpu.VMEM((3, 128, 512), F32),
            pltpu.VMEM((20, 8, 128), F32),
            pltpu.SemaphoreType.DMA((8,)),
            pltpu.SemaphoreType.DMA((count,)),
            pltpu.SemaphoreType.DMA((count,)),
            pltpu.SemaphoreType.DMA((17,)),
            pltpu.SemaphoreType.DMA((17,)),
            pltpu.SemaphoreType.DMA((2,)),
            pltpu.SemaphoreType.DMA((2,)),
        ],
        compiler_params=pltpu.CompilerParams(collective_id=0, has_side_effects=True, vmem_limit_bytes=60 * 1024 * 1024),
    )(
        tokens.reshape(64, 8192),
        norm_gain.reshape(1, 8192),
        jnp.transpose(master_weight, (1, 0, 2)),
        short_filter,
        medium_filter,
        medium_skip.reshape(1, 512),
        jnp.asarray(ftab),
        jnp.asarray(gtab),
    )
    return mixed[None], peak


def solution(mesh):
    placed = (
        P("dp", ("seq", "tensor"), None),
        P(),
        P(("dp", "seq"), None, "tensor"),
        P(None, None, "tensor"),
        P(None, "tensor"),
        P("tensor"),
    )
    return jax.shard_map(
        shards,
        mesh=mesh,
        in_specs=placed,
        out_specs=(P("dp", "seq", "tensor"), P()),
        check_vma=False,
    )
```

```python
import functools
import heapq

import jax
import jax.numpy as jnp
import numpy as np
from jax import lax
from jax.experimental import pallas as pl
from jax.experimental.pallas import tpu as pltpu
from jax.sharding import PartitionSpec as P

MESH = pl.DeviceIdType.MESH
F32 = jnp.float32
BF16 = jnp.bfloat16
eps_norm = 1e-06
eps_peak = 1e-06
grid_top = 448.0

ring_slots = [0, 1, -1, 2, -2, 3, -3, 4]
slot_of = {d: s for s, d in enumerate(ring_slots)}
slot_of[-4] = slot_of[4]

chunks = [(0, None), (-1, None), (1, None), (2, 0), (2, -1), (2, 1), (2, 2)]


def wrap4(d):
    return {-2: 2, 3: -1, -3: 1}.get(d, d)


def plan_messages():
    msgs = {}
    for ci, (dy, dx) in enumerate(chunks):
        size = 64 * 2 * (2048 if dx is None else 512)
        for sign, link in ((1, "zp"), (-1, "zm")):
            for hop in range(4):
                dep = [(link, ci, hop - 1)] if hop else []
                sub = None if hop < 3 else (0 if sign == 1 else 1)
                msgs[(link, ci, hop)] = (link, size if hop < 3 else size // 2, dep, ("tok", -sign * hop, sub, ci))
    quarter = 64 * 1536 * 2

    def ring(half, axis, fixed, need):
        first = 2 * half
        for sign in (1, -1):
            link = axis + ("p" if sign == 1 else "m")
            order = (first, first + 1) if sign == 1 else (first + 1, first)
            names = [(half, link, fixed, n) for n in range(3)]
            place = lambda d: (0, d) if axis == "x" else (d, 0)
            spot = lambda d: (fixed, d) if axis == "x" else (d, fixed)
            for n in range(2):
                msgs[names[n]] = (link, quarter, need(order[n]), ("w",) + spot(0) + (order[n],))
            msgs[names[2]] = (link, quarter, [names[0]], ("w",) + spot(-sign) + (order[0],))

    def arrival(half, axis, fixed, d, q):
        first = 2 * half
        if d == 0:
            return []
        if d == 2:
            return [(half, axis + ("p" if q == first else "m"), fixed, 2)]
        sign = -d
        order = (first, first + 1) if sign == 1 else (first + 1, first)
        return [(half, axis + ("p" if sign == 1 else "m"), fixed, order.index(q))]

    ring(0, "x", 0, lambda q: [])
    ring(1, "y", 0, lambda q: [])
    got = {}
    for d in (0, -1, 1, 2):
        for q in (0, 1):
            got[(0, d, q)] = arrival(0, "x", 0, d, q)
        for q in (2, 3):
            got[(d, 0, q)] = arrival(1, "y", 0, d, q)
    second = {}
    for d in (0, -1, 1, 2):
        tag0, tag1 = ("s", d), ("s", d)

        def ring2(half, axis, across):
            first = 2 * half
            for sign in (1, -1):
                link = axis + ("p" if sign == 1 else "m")
                order = (first, first + 1) if sign == 1 else (first + 1, first)
                names = [(half, link, ("s", across), n) for n in range(3)]
                spot = lambda e: (across, e) if axis == "x" else (e, across)
                for n in range(2):
                    key = spot(0) + (order[n],)
                    msgs[names[n]] = (link, quarter, got[key], ("w",) + spot(0) + (order[n],))
                msgs[names[2]] = (link, quarter, [names[0]], ("w",) + spot(-sign) + (order[0],))
            for e in (-1, 1, 2):
                for q in (first, first + 1):
                    if e == 2:
                        name = (half, axis + ("p" if q == first else "m"), ("s", across), 2)
                    else:
                        sign = -e
                        order = (first, first + 1) if sign == 1 else (first + 1, first)
                        name = (half, axis + ("p" if sign == 1 else "m"), ("s", across), order.index(q))
                    second[spot(e) + (q,)] = [name]

        ring2(0, "y", d)
        ring2(1, "x", d)
    got.update(second)
    for dy in (0, -1, 1, 2):
        for dx in (0, -1, 1, 2):
            for h in (0, 1):
                need = got[(dy, dx, 2 * h)] + got[(dy, dx, 2 * h + 1)]
                msgs[("pair", dy, dx, h)] = ("core", 2 * quarter, need, ("half", dy, dx, h))
    return msgs, got


def urgency(name):
    if name[0] in ("zp", "zm"):
        _, ci, hop = name
        at = (0.0, 4.0, 8.0, 12.0, 13.0, 14.0, 15.0)[ci]
        return at + 2.0 * hop if hop or ci > 2 else ci - 10.0
    if name[0] == "pair":
        return 0.0
    half, _, across, n = name
    if not isinstance(across, tuple):
        return n * 0.1
    d = {0: 0, -1: 1, 1: 2, 2: 3}[across[1]]
    if half == 0:
        return 10.0 + d * 0.1 + (10.0 if n == 2 else 0.0)
    return 10.0 + 4.0 * d + n * 0.1


def timeline(msgs):
    rate = {"z": 46.0e3, "x": 46.0e3, "y": 46.0e3, "c": 250.0e3}
    children = {}
    for name, (_, _, need, _) in msgs.items():
        for dep in need:
            children.setdefault(dep, []).append(name)
    rank = {name: i for i, name in enumerate(msgs)}
    left = {name: len(need) for name, (_, _, need, _) in msgs.items()}
    ready = {name: 0.0 for name in msgs}
    queue = {link: [] for link in ("zp", "zm", "xp", "xm", "yp", "ym", "core")}
    heap = []
    for name, (link, _, need, _) in msgs.items():
        if not need:
            ready[name] = 4.0 if link[0] == "z" else 14.0
            heapq.heappush(heap, (ready[name], 0, rank[name], name))
    busy = set()
    arrive, issue = {}, {}

    def serve(link, now):
        if link in busy or not queue[link]:
            return
        _, _, name = heapq.heappop(queue[link])
        busy.add(link)
        done = now + msgs[name][1] / rate[link[0]]
        arrive[name] = done + 1.5
        issue[name] = now
        heapq.heappush(heap, (done, 1, rank[name], name))
        for child in children.get(name, ()):
            left[child] -= 1
            ready[child] = max(ready[child], arrive[name])
            if left[child] == 0:
                heapq.heappush(heap, (ready[child], 0, rank[child], child))

    while heap:
        now, kind, _, name = heapq.heappop(heap)
        link = msgs[name][0]
        if kind == 1:
            busy.discard(link)
        else:
            heapq.heappush(queue[link], (urgency(name), rank[name], name))
        if not heap or heap[0][0] > now:
            for key in queue:
                serve(key, now)
    lead = 6.0
    early = {name: max(ready[name], issue[name] - lead) for name in msgs}
    return early, arrive


def plan():
    msgs, got = plan_messages()
    issue, arrive = timeline(msgs)
    tok_need = {}
    for ci, (dy, dx) in enumerate(chunks):
        tok_need[(dy, dx)] = [(link, ci, hop) for link in ("zp", "zm") for hop in range(4)]
    tasks = []
    for dy in (0, -1, 1, 2):
        for dx in (0, -1, 1, 2):
            need = list(tok_need[(dy, None)] if (dy, None) in tok_need else tok_need[(dy, dx)])
            for q in range(4):
                need += got[(dy, dx, q)]
            need += [("pair", dy, dx, h) for h in (0, 1)]
            tasks.append((max(arrive[n] for n in need), need, dy, dx))
    tasks.sort(key=lambda t: t[0])
    events = [(issue[name], 0, i, ("send", name)) for i, name in enumerate(msgs)]
    at = 0.0
    for i, (when, need, dy, dx) in enumerate(tasks):
        at = max(at, when + (3.0 if dy != 2 else 0.0))
        events.append((at, 1, i, ("dot", need, dy, dx)))
        at += 1.3
    events.sort(key=lambda e: e[:3])
    placed, order = set(), []
    for event in events:
        if event[3][0] == "send":
            assert all(dep in placed for dep in msgs[event[3][1]][2])
            placed.add(event[3][1])
        order.append(event[3])
    return msgs, order, at


def dft_tables():
    n = np.arange(256)
    k = np.arange(128)[:, None]
    angle = 2.0 * np.pi * ((k * n[None, :]) % 256) / 256.0
    lower = np.sin(angle)
    lower[0] = np.cos(np.pi * n)
    full = np.concatenate([np.cos(angle), lower], axis=0)

    def split(a):
        a = a.astype(np.float32)
        hi = a.astype(BF16)
        lo = (a - hi.astype(np.float32)).astype(BF16)
        return np.stack([hi, lo])

    return split(full), split(full[:, 128:].T)


def round_grid(v):
    m = jnp.abs(v)
    t = m * F32(8388609.0)
    top = t - t * F32(1.0 - 2.0**-24)
    quantum = jnp.maximum(top, F32(2.0**-6)) * F32(0.125)
    magic = quantum * F32(1.5 * 2.0**23)
    r = (m + magic) - magic
    r = jnp.where(m - r == quantum * F32(0.5), r + quantum, r)
    return jnp.where(v < 0, -r, r)


def kernel(
    program,
    tok_hbm, gain_hbm, w_hbm, sf_hbm, mf_hbm, skip_hbm, f_hbm, g_hbm,
    out_ref, peak_ref,
    tok_in, gain, w_in, sf, mf, skip, fmat, gmat,
    a_all, w_all, acc, feat, gext, hspec, peaks,
    local_sem, send_sem, recv_sem, pk_send, pk_recv, halo_send, halo_recv,
):
    msgs, events, ids = program
    y = lax.axis_index("dp")
    s = lax.axis_index("seq")
    z = lax.axis_index("tensor")
    x, c = s // 2, s % 2

    ins = [(w_hbm, w_in), (tok_hbm, tok_in), (gain_hbm, gain), (mf_hbm, mf), (f_hbm, fmat), (g_hbm, gmat), (sf_hbm, sf), (skip_hbm, skip)]
    loads = [pltpu.make_async_copy(src, dst, local_sem.at[i]) for i, (src, dst) in enumerate(ins)]
    for i in (1, 2, 0, 3, 4, 5, 6, 7):
        loads[i].start()

    def dev(dy, ds, dz):
        return ((y + dy) % 4, ds, (z + dz) % 8)

    barrier = pltpu.get_barrier_semaphore()
    peers = [dev(0, s, k) for k in range(1, 8)] + [dev(dy, (s + k) % 8, 0) for dy in range(4) for k in range(8) if dy or k]
    for peer in peers:
        pl.semaphore_signal(barrier, inc=1, device_id=peer, device_id_type=MESH)

    loads[1].wait()
    loads[2].wait()
    root = []
    for r in range(0, 64, 16):
        v = tok_in[r : r + 16, :].astype(F32)
        root.append(lax.rsqrt(jnp.sum(v * v, axis=1, keepdims=True) * F32(1.0 / 8192) + F32(eps_norm)))

    def norm_columns(dy):
        cols = pl.ds(pl.multiple_of(((y + dy) % 4) * 2048, 2048), 2048)
        for r in range(0, 64, 16):
            a_all[r : r + 16, cols] = (tok_in[r : r + 16, cols].astype(F32) * root[r // 16] * gain[:, cols]).astype(BF16)

    norm_columns(0)

    def peak_round(src, base, targets):
        copies = []
        for i, target in enumerate(targets):
            copies.append(
                pltpu.make_async_remote_copy(
                    src_ref=peaks.at[src], dst_ref=peaks.at[2 + base + i],
                    send_sem=pk_send.at[base + i], recv_sem=pk_recv.at[base + i],
                    device_id=target, device_id_type=MESH,
                )
            )
        for copy in copies:
            copy.start()
        return copies

    def peak_finish(copies, src, base):
        best = peaks[src]
        for i, copy in enumerate(copies):
            copy.wait_recv()
            best = jnp.maximum(best, peaks[2 + base + i])
        return best

    def w_row(dy, dx, parity):
        return (((y + dy) % 4) * 8 + ((x + dx) % 4) * 2 + parity) * 256

    def message(name):
        link, _, _, place = msgs[name]
        if place[0] == "tok":
            _, d, sub, ci = place
            step = 1 if link == "zp" else -1
            off, rows = (0, 64) if sub is None else (32 * sub, 32)
            here = slot_of[d] * 64 + off
            there = slot_of[d - step] * 64 + off
            dy, dx = chunks[ci]
            if dx is None:
                cols = pl.ds(pl.multiple_of(((y + dy) % 4) * 2048, 2048), 2048)
            else:
                cols = pl.ds(pl.multiple_of(w_row(dy, dx, 0), 512), 512)
            src, dst = a_all.at[here : here + rows, cols], a_all.at[there : there + rows, cols]
            target = dev(0, s, step)
        elif place[0] == "w":
            _, dy, dx, q = place
            row = pl.multiple_of(w_row(dy, dx, c) + 64 * q, 64)
            src = dst = w_all.at[pl.ds(row, 64), :]
            if link[0] == "x":
                target = dev(0, (s + (2 if link[1] == "p" else 6)) % 8, 0)
            else:
                target = dev(1 if link[1] == "p" else 3, s, 0)
        else:
            _, dy, dx, h = place
            row = pl.multiple_of(w_row(dy, dx, c) + 128 * h, 128)
            src = dst = w_all.at[pl.ds(row, 128), :]
            target = (y, x * 2 + 1 - c, z)
        i = ids[name]
        return pltpu.make_async_remote_copy(
            src_ref=src, dst_ref=dst, send_sem=send_sem.at[i], recv_sem=recv_sem.at[i], device_id=target, device_id_type=MESH
        )

    copies = {name: message(name) for name in msgs}
    arrived = set()
    started = [(link, ci, 0) for ci in range(3) for link in ("zp", "zm")]

    def need(names):
        for name in names:
            if name not in arrived:
                arrived.add(name)
                copies[name].wait_recv()

    pl.semaphore_wait(barrier, len(peers))
    for name in started[:2]:
        copies[name].start()

    loads[0].wait()
    top = jnp.zeros((8, 512), F32)
    part = [jnp.zeros((8, 512), F32) for _ in range(4)]
    for k in range(3):
        for r in range(0, 256, 32):
            for j in range(4):
                part[j] = jnp.maximum(part[j], jnp.abs(w_in[k, r + 8 * j : r + 8 * j + 8, :]))
    top = jnp.maximum(jnp.maximum(part[0], part[1]), jnp.maximum(part[2], part[3]))
    top = jnp.max(jnp.max(top, axis=0, keepdims=True), axis=1, keepdims=True)
    peaks[0] = jnp.broadcast_to(top, (8, 128))

    round0 = peak_round(0, 0, peers[:7])
    norm_columns(-1)
    for name in started[2:4]:
        copies[name].start()
    norm_columns(1)
    for name in started[4:6]:
        copies[name].start()
    norm_columns(2)
    peaks[1] = peak_finish(round0, 0, 0)
    round1 = peak_round(1, 7, peers[7:])
    peak = peak_finish(round1, 1, 7)
    peak_ref[0] = jnp.max(peak)

    ratio = F32(grid_top) / (peak + F32(eps_peak))
    factor = jnp.ones((8, 128), F32)
    inverse = jnp.ones((8, 128), F32)
    for p in (16, 8, 4, 2, 1):
        larger = factor * F32(2.0**p)
        over = ratio >= larger
        factor = jnp.where(over, larger, factor)
        inverse = jnp.where(over, inverse * F32(2.0**-p), inverse)
    factor = jnp.broadcast_to(factor[0:1, 0:1], (1, 512))
    inverse = jnp.broadcast_to(inverse[0:1, 0:1], (1, 512))
    own = pl.multiple_of(w_row(0, 0, c), 256)

    def recast(i, carry):
        r = pl.multiple_of(i * 32, 32)
        for k in range(3):
            w_all[pl.ds(own + r, 32), 512 * k : 512 * k + 512] = round_grid(w_in[k, pl.ds(r, 32), :] * factor).astype(BF16)
        return carry

    lax.fori_loop(0, 8, recast, 0)

    def spectrum():
        for load in loads[3:]:
            load.wait()
        taps = mf[...]
        h = jnp.dot(fmat[0, :, 0:128], taps, preferred_element_type=F32) + jnp.dot(fmat[1, :, 0:128], taps, preferred_element_type=F32)
        first = lax.broadcasted_iota(jnp.int32, (128, 512), 0) == 0
        scale = jnp.where(first, F32(1.0 / 256), F32(2.0 / 256))
        hc, hs = h[0:128] * scale, h[128:256] * scale
        hspec[0] = hc
        hspec[1] = jnp.where(first, F32(0.0), hs)
        hspec[2] = jnp.where(first, hs, hc)

    def product(dy, dx, fresh):
        k0 = pl.multiple_of(w_row(dy, dx, 0), 512)

        def column(i, carry):
            n = pl.multiple_of(i * 512, 512)
            got = jnp.dot(a_all[:, pl.ds(k0, 512)], w_all[pl.ds(k0, 512), pl.ds(n, 512)], preferred_element_type=F32)
            if fresh:
                acc[:, pl.ds(n, 512)] = got
            else:
                acc[:, pl.ds(n, 512)] += got
            return carry

        lax.fori_loop(0, 3, column, 0)

    fresh = True
    ready = False
    for event in events:
        if event[0] == "send":
            name = event[1]
            if name in started:
                continue
            need(msgs[name][2])
            copies[name].start()
            if not ready and msgs[name][2]:
                ready = True
                spectrum()
        else:
            _, names, dy, dx = event
            need(names)
            product(dy, dx, fresh)
            fresh = False

    inverse_row = inverse
    for slot, d in enumerate(ring_slots):
        row = pl.multiple_of(8 + 64 * ((z + d) % 8), 8)
        for k in range(3):
            cols = slice(512 * k, 512 * k + 512)
            feat[pl.ds(row, 64), cols] = (acc[64 * slot : 64 * slot + 64, cols] * inverse_row).astype(BF16).astype(F32)

    after = (y, (s + 1) % 8, z)
    rim = pltpu.make_async_remote_copy(
        src_ref=feat.at[512:520, :], dst_ref=feat.at[0:8, :], send_sem=halo_send.at[0], recv_sem=halo_recv.at[0],
        device_id=after, device_id_type=MESH,
    )
    rim.start()

    def short(k, lo, rows):
        total = jnp.zeros((rows, 512), F32)
        for j in range(3):
            total = total + sf[k, j : j + 1, :] * feat[8 + lo - j : 8 + lo - j + rows, 512 * k : 512 * k + 512]
        return total

    def gate(lo, rows):
        gext[128 + lo : 128 + lo + rows, :] = (short(1, lo, rows) * short(2, lo, rows)).astype(BF16)

    gate(384, 128)
    edge = pltpu.make_async_remote_copy(
        src_ref=gext.at[512:640, :], dst_ref=gext.at[0:128, :], send_sem=halo_send.at[1], recv_sem=halo_recv.at[1],
        device_id=after, device_id_type=MESH,
    )
    edge.start()
    gate(256, 128)
    gate(128, 128)
    gate(16, 112)

    def mix(b):
        lo = 128 * b
        e = gext[lo : lo + 256, :]
        t = jnp.dot(fmat[0], e, preferred_element_type=F32) + jnp.dot(fmat[1], e, preferred_element_type=F32)
        tc, ts = t[0:128], t[128:256]
        pc = tc * hspec[0] - ts * hspec[1]
        ps = tc * hspec[1] + ts * hspec[2]
        p = jnp.concatenate([pc, ps], axis=0)
        ph = p.astype(BF16)
        pl_ = (p - ph.astype(F32)).astype(BF16)
        f = jnp.dot(gmat[0], ph, preferred_element_type=F32)
        f = f + jnp.dot(gmat[0], pl_, preferred_element_type=F32)
        f = f + jnp.dot(gmat[1], ph, preferred_element_type=F32)
        f = f + skip[...] * e[128:256].astype(F32)
        out_ref[lo : lo + 128, :] = (short(0, lo, 128) * f).astype(BF16)

    mix(3)
    mix(2)
    rim.wait_recv()
    edge.wait_recv()

    @pl.when(s == 0)
    def _():
        feat[0:8, :] = jnp.zeros((8, 1536), F32)
        gext[0:128, :] = jnp.zeros((128, 512), BF16)

    gate(0, 16)
    mix(1)
    mix(0)
    rim.wait_send()
    edge.wait_send()
    for copy in round0 + round1:
        copy.wait_send()
    for copy in copies.values():
        copy.wait_send()


def shards(tokens, norm_gain, master_weight, short_filter, medium_filter, medium_skip):
    msgs, events, _ = plan()
    ids = {name: i for i, name in enumerate(msgs)}
    ftab, gtab = dft_tables()
    count = len(msgs)
    any_space = pl.BlockSpec(memory_space=pl.ANY)
    mixed, peak = pl.pallas_call(
        functools.partial(kernel, (msgs, events, ids)),
        out_shape=(jax.ShapeDtypeStruct((512, 512), BF16), jax.ShapeDtypeStruct((1,), F32)),
        in_specs=[any_space] * 8,
        out_specs=(pl.BlockSpec(memory_space=pltpu.VMEM), pl.BlockSpec(memory_space=pltpu.SMEM)),
        scratch_shapes=[
            pltpu.VMEM((64, 8192), BF16),
            pltpu.VMEM((1, 8192), F32),
            pltpu.VMEM((3, 256, 512), F32),
            pltpu.VMEM((3, 3, 512), F32),
            pltpu.VMEM((128, 512), BF16),
            pltpu.VMEM((1, 512), F32),
            pltpu.VMEM((2, 256, 256), BF16),
            pltpu.VMEM((2, 128, 256), BF16),
            pltpu.VMEM((512, 8192), BF16),
            pltpu.VMEM((8192, 1536), BF16),
            pltpu.VMEM((512, 1536), F32),
            pltpu.VMEM((520, 1536), F32),
            pltpu.VMEM((640, 512), BF16),
            pltpu.VMEM((3, 128, 512), F32),
            pltpu.VMEM((40, 8, 128), F32),
            pltpu.SemaphoreType.DMA((8,)),
            pltpu.SemaphoreType.DMA((count,)),
            pltpu.SemaphoreType.DMA((count,)),
            pltpu.SemaphoreType.DMA((38,)),
            pltpu.SemaphoreType.DMA((38,)),
            pltpu.SemaphoreType.DMA((2,)),
            pltpu.SemaphoreType.DMA((2,)),
        ],
        compiler_params=pltpu.CompilerParams(collective_id=0, has_side_effects=True, vmem_limit_bytes=60 * 1024 * 1024),
    )(
        tokens.reshape(64, 8192),
        norm_gain.reshape(1, 8192),
        jnp.transpose(master_weight, (1, 0, 2)),
        short_filter,
        medium_filter,
        medium_skip.reshape(1, 512),
        jnp.asarray(ftab),
        jnp.asarray(gtab),
    )
    return mixed[None], peak


def solution(mesh):
    placed = (
        P("dp", ("seq", "tensor"), None),
        P(),
        P(("dp", "seq"), None, "tensor"),
        P(None, None, "tensor"),
        P(None, "tensor"),
        P("tensor"),
    )
    return jax.shard_map(
        shards,
        mesh=mesh,
        in_specs=placed,
        out_specs=(P("dp", "seq", "tensor"), P()),
        check_vma=False,
    )
```

```python
import functools
import heapq

import jax
import jax.numpy as jnp
import numpy as np
from jax import lax
from jax.experimental import pallas as pl
from jax.experimental.pallas import tpu as pltpu
from jax.sharding import PartitionSpec as P

MESH = pl.DeviceIdType.MESH
F32 = jnp.float32
BF16 = jnp.bfloat16
eps_norm = 1e-06
eps_peak = 1e-06
grid_top = 448.0

ring_slots = [0, 1, -1, 2, -2, 3, -3, 4]
slot_of = {d: s for s, d in enumerate(ring_slots)}
slot_of[-4] = slot_of[4]

chunks = [(0, None), (-1, None), (1, None), (2, 0), (2, -1), (2, 1), (2, 2)]


def wrap4(d):
    return {-2: 2, 3: -1, -3: 1}.get(d, d)


def plan_messages():
    msgs = {}
    for ci, (dy, dx) in enumerate(chunks):
        size = 64 * 2 * (2048 if dx is None else 512)
        for sign, link in ((1, "zp"), (-1, "zm")):
            for hop in range(4):
                dep = [(link, ci, hop - 1)] if hop else []
                sub = None if hop < 3 else (0 if sign == 1 else 1)
                msgs[(link, ci, hop)] = (link, size if hop < 3 else size // 2, dep, ("tok", -sign * hop, sub, ci))
    quarter = 64 * 1536 * 2

    def ring(half, axis, fixed, need):
        first = 2 * half
        for sign in (1, -1):
            link = axis + ("p" if sign == 1 else "m")
            order = (first, first + 1) if sign == 1 else (first + 1, first)
            names = [(half, link, fixed, n) for n in range(3)]
            place = lambda d: (0, d) if axis == "x" else (d, 0)
            spot = lambda d: (fixed, d) if axis == "x" else (d, fixed)
            for n in range(2):
                msgs[names[n]] = (link, quarter, need(order[n]), ("w",) + spot(0) + (order[n],))
            msgs[names[2]] = (link, quarter, [names[0]], ("w",) + spot(-sign) + (order[0],))

    def arrival(half, axis, fixed, d, q):
        first = 2 * half
        if d == 0:
            return []
        if d == 2:
            return [(half, axis + ("p" if q == first else "m"), fixed, 2)]
        sign = -d
        order = (first, first + 1) if sign == 1 else (first + 1, first)
        return [(half, axis + ("p" if sign == 1 else "m"), fixed, order.index(q))]

    ring(0, "x", 0, lambda q: [])
    ring(1, "y", 0, lambda q: [])
    got = {}
    for d in (0, -1, 1, 2):
        for q in (0, 1):
            got[(0, d, q)] = arrival(0, "x", 0, d, q)
        for q in (2, 3):
            got[(d, 0, q)] = arrival(1, "y", 0, d, q)
    second = {}
    for d in (0, -1, 1, 2):
        tag0, tag1 = ("s", d), ("s", d)

        def ring2(half, axis, across):
            first = 2 * half
            for sign in (1, -1):
                link = axis + ("p" if sign == 1 else "m")
                order = (first, first + 1) if sign == 1 else (first + 1, first)
                names = [(half, link, ("s", across), n) for n in range(3)]
                spot = lambda e: (across, e) if axis == "x" else (e, across)
                for n in range(2):
                    key = spot(0) + (order[n],)
                    msgs[names[n]] = (link, quarter, got[key], ("w",) + spot(0) + (order[n],))
                msgs[names[2]] = (link, quarter, [names[0]], ("w",) + spot(-sign) + (order[0],))
            for e in (-1, 1, 2):
                for q in (first, first + 1):
                    if e == 2:
                        name = (half, axis + ("p" if q == first else "m"), ("s", across), 2)
                    else:
                        sign = -e
                        order = (first, first + 1) if sign == 1 else (first + 1, first)
                        name = (half, axis + ("p" if sign == 1 else "m"), ("s", across), order.index(q))
                    second[spot(e) + (q,)] = [name]

        ring2(0, "y", d)
        ring2(1, "x", d)
    got.update(second)
    for dy in (0, -1, 1, 2):
        for dx in (0, -1, 1, 2):
            for h in (0, 1):
                need = got[(dy, dx, 2 * h)] + got[(dy, dx, 2 * h + 1)]
                msgs[("pair", dy, dx, h)] = ("core", 2 * quarter, need, ("half", dy, dx, h))
    return msgs, got


def urgency(name):
    if name[0] in ("zp", "zm"):
        _, ci, hop = name
        at = (0.0, 4.0, 8.0, 12.0, 13.0, 14.0, 15.0)[ci]
        return at + 2.0 * hop if hop or ci > 2 else ci - 10.0
    if name[0] == "pair":
        return 0.0
    half, _, across, n = name
    if not isinstance(across, tuple):
        return n * 0.1
    d = {0: 0, -1: 1, 1: 2, 2: 3}[across[1]]
    if half == 0:
        return 10.0 + d * 0.1 + (10.0 if n == 2 else 0.0)
    return 10.0 + 4.0 * d + n * 0.1


def timeline(msgs):
    rate = {"z": 46.0e3, "x": 46.0e3, "y": 46.0e3, "c": 250.0e3}
    children = {}
    for name, (_, _, need, _) in msgs.items():
        for dep in need:
            children.setdefault(dep, []).append(name)
    rank = {name: i for i, name in enumerate(msgs)}
    left = {name: len(need) for name, (_, _, need, _) in msgs.items()}
    ready = {name: 0.0 for name in msgs}
    queue = {link: [] for link in ("zp", "zm", "xp", "xm", "yp", "ym", "core")}
    heap = []
    for name, (link, _, need, _) in msgs.items():
        if not need:
            ready[name] = 4.0 if link[0] == "z" else 14.0
            heapq.heappush(heap, (ready[name], 0, rank[name], name))
    busy = set()
    arrive, issue = {}, {}

    def serve(link, now):
        if link in busy or not queue[link]:
            return
        _, _, name = heapq.heappop(queue[link])
        busy.add(link)
        done = now + msgs[name][1] / rate[link[0]]
        arrive[name] = done + 1.5
        issue[name] = now
        heapq.heappush(heap, (done, 1, rank[name], name))
        for child in children.get(name, ()):
            left[child] -= 1
            ready[child] = max(ready[child], arrive[name])
            if left[child] == 0:
                heapq.heappush(heap, (ready[child], 0, rank[child], child))

    while heap:
        now, kind, _, name = heapq.heappop(heap)
        link = msgs[name][0]
        if kind == 1:
            busy.discard(link)
        else:
            heapq.heappush(queue[link], (urgency(name), rank[name], name))
        if not heap or heap[0][0] > now:
            for key in queue:
                serve(key, now)
    lead = 1.5
    early = {name: max(ready[name], issue[name] - lead) for name in msgs}
    return early, arrive


def plan():
    msgs, got = plan_messages()
    issue, arrive = timeline(msgs)
    tok_need = {}
    for ci, (dy, dx) in enumerate(chunks):
        tok_need[(dy, dx)] = [(link, ci, hop) for link in ("zp", "zm") for hop in range(4)]
    tasks = []
    for dy in (0, -1, 1, 2):
        for dx in (0, -1, 1, 2):
            need = list(tok_need[(dy, None)] if (dy, None) in tok_need else tok_need[(dy, dx)])
            for q in range(4):
                need += got[(dy, dx, q)]
            need += [("pair", dy, dx, h) for h in (0, 1)]
            tasks.append((max(arrive[n] for n in need), need, dy, dx))
    tasks.sort(key=lambda t: t[0])
    events = [(issue[name], 0, i, ("send", name)) for i, name in enumerate(msgs)]
    at = 0.0
    for i, (when, need, dy, dx) in enumerate(tasks):
        at = max(at, when)
        events.append((at, 1, i, ("dot", need, dy, dx)))
        at += 1.3
    events.sort(key=lambda e: e[:3])
    placed, order = set(), []
    for event in events:
        if event[3][0] == "send":
            assert all(dep in placed for dep in msgs[event[3][1]][2])
            placed.add(event[3][1])
        order.append(event[3])
    return msgs, order, at


def dft_tables():
    n = np.arange(256)
    k = np.arange(128)[:, None]
    angle = 2.0 * np.pi * ((k * n[None, :]) % 256) / 256.0
    lower = np.sin(angle)
    lower[0] = np.cos(np.pi * n)
    full = np.concatenate([np.cos(angle), lower], axis=0)

    def split(a):
        a = a.astype(np.float32)
        hi = a.astype(BF16)
        lo = (a - hi.astype(np.float32)).astype(BF16)
        return np.stack([hi, lo])

    return split(full), split(full[:, 128:].T)


def round_grid(v):
    m = jnp.abs(v)
    t = m * F32(8388609.0)
    top = t - t * F32(1.0 - 2.0**-24)
    quantum = jnp.maximum(top, F32(2.0**-6)) * F32(0.125)
    magic = quantum * F32(1.5 * 2.0**23)
    r = (m + magic) - magic
    r = jnp.where(m - r == quantum * F32(0.5), r + quantum, r)
    return jnp.where(v < 0, -r, r)


def kernel(
    program,
    tok_hbm, gain_hbm, w_hbm, sf_hbm, mf_hbm, skip_hbm, f_hbm, g_hbm,
    out_ref, peak_ref,
    tok_in, gain, w_in, sf, mf, skip, fmat, gmat,
    a_all, w_all, acc, feat, gext, hspec, peaks,
    local_sem, send_sem, recv_sem, pk_send, pk_recv, halo_send, halo_recv,
):
    msgs, events, ids = program
    y = lax.axis_index("dp")
    s = lax.axis_index("seq")
    z = lax.axis_index("tensor")
    x, c = s // 2, s % 2

    ins = [(w_hbm, w_in), (tok_hbm, tok_in), (gain_hbm, gain), (mf_hbm, mf), (f_hbm, fmat), (g_hbm, gmat), (sf_hbm, sf), (skip_hbm, skip)]
    loads = [pltpu.make_async_copy(src, dst, local_sem.at[i]) for i, (src, dst) in enumerate(ins)]
    for i in (1, 2, 0, 3, 4, 5, 6, 7):
        loads[i].start()

    def dev(dy, ds, dz):
        return ((y + dy) % 4, ds, (z + dz) % 8)

    barrier = pltpu.get_barrier_semaphore()
    peers = [dev(0, s, k) for k in range(1, 8)] + [dev(dy, (s + k) % 8, 0) for dy in range(4) for k in range(8) if dy or k]
    for peer in peers:
        pl.semaphore_signal(barrier, inc=1, device_id=peer, device_id_type=MESH)

    loads[1].wait()
    loads[2].wait()
    root = []
    for r in range(0, 64, 16):
        v = tok_in[r : r + 16, :].astype(F32)
        root.append(lax.rsqrt(jnp.sum(v * v, axis=1, keepdims=True) * F32(1.0 / 8192) + F32(eps_norm)))

    def norm_columns(dy):
        cols = pl.ds(pl.multiple_of(((y + dy) % 4) * 2048, 2048), 2048)
        for r in range(0, 64, 16):
            a_all[r : r + 16, cols] = (tok_in[r : r + 16, cols].astype(F32) * root[r // 16] * gain[:, cols]).astype(BF16)

    norm_columns(0)

    def peak_round(src, base, targets):
        copies = []
        for i, target in enumerate(targets):
            copies.append(
                pltpu.make_async_remote_copy(
                    src_ref=peaks.at[src], dst_ref=peaks.at[2 + base + i],
                    send_sem=pk_send.at[base + i], recv_sem=pk_recv.at[base + i],
                    device_id=target, device_id_type=MESH,
                )
            )
        for copy in copies:
            copy.start()
        return copies

    def peak_finish(copies, src, base):
        best = peaks[src]
        for i, copy in enumerate(copies):
            copy.wait_recv()
            best = jnp.maximum(best, peaks[2 + base + i])
        return best

    def w_row(dy, dx, parity):
        return (((y + dy) % 4) * 8 + ((x + dx) % 4) * 2 + parity) * 256

    def message(name):
        link, _, _, place = msgs[name]
        if place[0] == "tok":
            _, d, sub, ci = place
            step = 1 if link == "zp" else -1
            off, rows = (0, 64) if sub is None else (32 * sub, 32)
            here = slot_of[d] * 64 + off
            there = slot_of[d - step] * 64 + off
            dy, dx = chunks[ci]
            if dx is None:
                cols = pl.ds(pl.multiple_of(((y + dy) % 4) * 2048, 2048), 2048)
            else:
                cols = pl.ds(pl.multiple_of(w_row(dy, dx, 0), 512), 512)
            src, dst = a_all.at[here : here + rows, cols], a_all.at[there : there + rows, cols]
            target = dev(0, s, step)
        elif place[0] == "w":
            _, dy, dx, q = place
            row = pl.multiple_of(w_row(dy, dx, c) + 64 * q, 64)
            src = dst = w_all.at[pl.ds(row, 64), :]
            if link[0] == "x":
                target = dev(0, (s + (2 if link[1] == "p" else 6)) % 8, 0)
            else:
                target = dev(1 if link[1] == "p" else 3, s, 0)
        else:
            _, dy, dx, h = place
            row = pl.multiple_of(w_row(dy, dx, c) + 128 * h, 128)
            src = dst = w_all.at[pl.ds(row, 128), :]
            target = (y, x * 2 + 1 - c, z)
        i = ids[name]
        return pltpu.make_async_remote_copy(
            src_ref=src, dst_ref=dst, send_sem=send_sem.at[i], recv_sem=recv_sem.at[i], device_id=target, device_id_type=MESH
        )

    copies = {name: message(name) for name in msgs}
    arrived = set()
    started = [(link, ci, 0) for ci in range(3) for link in ("zp", "zm")]

    def need(names):
        for name in names:
            if name not in arrived:
                arrived.add(name)
                copies[name].wait_recv()

    pl.semaphore_wait(barrier, len(peers))
    for name in started[:2]:
        copies[name].start()

    loads[0].wait()
    top = jnp.zeros((8, 512), F32)
    part = [jnp.zeros((8, 512), F32) for _ in range(4)]
    for k in range(3):
        for r in range(0, 256, 32):
            for j in range(4):
                part[j] = jnp.maximum(part[j], jnp.abs(w_in[k, r + 8 * j : r + 8 * j + 8, :]))
    top = jnp.maximum(jnp.maximum(part[0], part[1]), jnp.maximum(part[2], part[3]))
    top = jnp.max(jnp.max(top, axis=0, keepdims=True), axis=1, keepdims=True)
    peaks[0] = jnp.broadcast_to(top, (8, 128))

    round0 = peak_round(0, 0, peers[:7])
    norm_columns(-1)
    for name in started[2:4]:
        copies[name].start()
    norm_columns(1)
    for name in started[4:6]:
        copies[name].start()
    norm_columns(2)
    peaks[1] = peak_finish(round0, 0, 0)
    round1 = peak_round(1, 7, peers[7:])
    peak = peak_finish(round1, 1, 7)
    peak_ref[0] = jnp.max(peak)

    ratio = F32(grid_top) / (peak + F32(eps_peak))
    factor = jnp.ones((8, 128), F32)
    inverse = jnp.ones((8, 128), F32)
    for p in (16, 8, 4, 2, 1):
        larger = factor * F32(2.0**p)
        over = ratio >= larger
        factor = jnp.where(over, larger, factor)
        inverse = jnp.where(over, inverse * F32(2.0**-p), inverse)
    factor = jnp.broadcast_to(factor[0:1, 0:1], (1, 512))
    inverse = jnp.broadcast_to(inverse[0:1, 0:1], (1, 512))
    own = pl.multiple_of(w_row(0, 0, c), 256)

    def recast(i, carry):
        r = pl.multiple_of(i * 32, 32)
        for k in range(3):
            w_all[pl.ds(own + r, 32), 512 * k : 512 * k + 512] = round_grid(w_in[k, pl.ds(r, 32), :] * factor).astype(BF16)
        return carry

    lax.fori_loop(0, 8, recast, 0)

    def spectrum():
        for load in loads[3:]:
            load.wait()
        taps = mf[...]
        h = jnp.dot(fmat[0, :, 0:128], taps, preferred_element_type=F32) + jnp.dot(fmat[1, :, 0:128], taps, preferred_element_type=F32)
        first = lax.broadcasted_iota(jnp.int32, (128, 512), 0) == 0
        scale = jnp.where(first, F32(1.0 / 256), F32(2.0 / 256))
        hc, hs = h[0:128] * scale, h[128:256] * scale
        hspec[0] = hc
        hspec[1] = jnp.where(first, F32(0.0), hs)
        hspec[2] = jnp.where(first, hs, hc)

    def product(dy, dx, fresh):
        k0 = pl.multiple_of(w_row(dy, dx, 0), 512)

        def column(i, carry):
            n = pl.multiple_of(i * 512, 512)
            got = jnp.dot(a_all[:, pl.ds(k0, 512)], w_all[pl.ds(k0, 512), pl.ds(n, 512)], preferred_element_type=F32)
            if fresh:
                acc[:, pl.ds(n, 512)] = got
            else:
                acc[:, pl.ds(n, 512)] += got
            return carry

        lax.fori_loop(0, 3, column, 0)

    fresh = True
    ready = False
    for event in events:
        if event[0] == "send":
            name = event[1]
            if name in started:
                continue
            need(msgs[name][2])
            copies[name].start()
            if not ready and msgs[name][2]:
                ready = True
                spectrum()
        else:
            _, names, dy, dx = event
            need(names)
            product(dy, dx, fresh)
            fresh = False

    inverse_row = inverse
    for slot, d in enumerate(ring_slots):
        row = pl.multiple_of(8 + 64 * ((z + d) % 8), 8)
        for k in range(3):
            cols = slice(512 * k, 512 * k + 512)
            feat[pl.ds(row, 64), cols] = (acc[64 * slot : 64 * slot + 64, cols] * inverse_row).astype(BF16).astype(F32)

    after = (y, (s + 1) % 8, z)
    rim = pltpu.make_async_remote_copy(
        src_ref=feat.at[512:520, :], dst_ref=feat.at[0:8, :], send_sem=halo_send.at[0], recv_sem=halo_recv.at[0],
        device_id=after, device_id_type=MESH,
    )
    rim.start()

    def short(k, lo, rows):
        total = jnp.zeros((rows, 512), F32)
        for j in range(3):
            total = total + sf[k, j : j + 1, :] * feat[8 + lo - j : 8 + lo - j + rows, 512 * k : 512 * k + 512]
        return total

    def gate(lo, rows):
        gext[128 + lo : 128 + lo + rows, :] = (short(1, lo, rows) * short(2, lo, rows)).astype(BF16)

    gate(384, 128)
    edge = pltpu.make_async_remote_copy(
        src_ref=gext.at[512:640, :], dst_ref=gext.at[0:128, :], send_sem=halo_send.at[1], recv_sem=halo_recv.at[1],
        device_id=after, device_id_type=MESH,
    )
    edge.start()
    gate(256, 128)
    gate(128, 128)
    gate(16, 112)

    def mix(b):
        lo = 128 * b
        e = gext[lo : lo + 256, :]
        t = jnp.dot(fmat[0], e, preferred_element_type=F32) + jnp.dot(fmat[1], e, preferred_element_type=F32)
        tc, ts = t[0:128], t[128:256]
        pc = tc * hspec[0] - ts * hspec[1]
        ps = tc * hspec[1] + ts * hspec[2]
        p = jnp.concatenate([pc, ps], axis=0)
        ph = p.astype(BF16)
        pl_ = (p - ph.astype(F32)).astype(BF16)
        f = jnp.dot(gmat[0], ph, preferred_element_type=F32)
        f = f + jnp.dot(gmat[0], pl_, preferred_element_type=F32)
        f = f + jnp.dot(gmat[1], ph, preferred_element_type=F32)
        f = f + skip[...] * e[128:256].astype(F32)
        out_ref[lo : lo + 128, :] = (short(0, lo, 128) * f).astype(BF16)

    mix(3)
    mix(2)
    rim.wait_recv()
    edge.wait_recv()

    @pl.when(s == 0)
    def _():
        feat[0:8, :] = jnp.zeros((8, 1536), F32)
        gext[0:128, :] = jnp.zeros((128, 512), BF16)

    gate(0, 16)
    mix(1)
    mix(0)
    rim.wait_send()
    edge.wait_send()
    for copy in round0 + round1:
        copy.wait_send()
    for copy in copies.values():
        copy.wait_send()


def shards(tokens, norm_gain, master_weight, short_filter, medium_filter, medium_skip):
    msgs, events, _ = plan()
    ids = {name: i for i, name in enumerate(msgs)}
    ftab, gtab = dft_tables()
    count = len(msgs)
    any_space = pl.BlockSpec(memory_space=pl.ANY)
    mixed, peak = pl.pallas_call(
        functools.partial(kernel, (msgs, events, ids)),
        out_shape=(jax.ShapeDtypeStruct((512, 512), BF16), jax.ShapeDtypeStruct((1,), F32)),
        in_specs=[any_space] * 8,
        out_specs=(pl.BlockSpec(memory_space=pltpu.VMEM), pl.BlockSpec(memory_space=pltpu.SMEM)),
        scratch_shapes=[
            pltpu.VMEM((64, 8192), BF16),
            pltpu.VMEM((1, 8192), F32),
            pltpu.VMEM((3, 256, 512), F32),
            pltpu.VMEM((3, 3, 512), F32),
            pltpu.VMEM((128, 512), BF16),
            pltpu.VMEM((1, 512), F32),
            pltpu.VMEM((2, 256, 256), BF16),
            pltpu.VMEM((2, 128, 256), BF16),
            pltpu.VMEM((512, 8192), BF16),
            pltpu.VMEM((8192, 1536), BF16),
            pltpu.VMEM((512, 1536), F32),
            pltpu.VMEM((520, 1536), F32),
            pltpu.VMEM((640, 512), BF16),
            pltpu.VMEM((3, 128, 512), F32),
            pltpu.VMEM((40, 8, 128), F32),
            pltpu.SemaphoreType.DMA((8,)),
            pltpu.SemaphoreType.DMA((count,)),
            pltpu.SemaphoreType.DMA((count,)),
            pltpu.SemaphoreType.DMA((38,)),
            pltpu.SemaphoreType.DMA((38,)),
            pltpu.SemaphoreType.DMA((2,)),
            pltpu.SemaphoreType.DMA((2,)),
        ],
        compiler_params=pltpu.CompilerParams(collective_id=0, has_side_effects=True, vmem_limit_bytes=60 * 1024 * 1024),
    )(
        tokens.reshape(64, 8192),
        norm_gain.reshape(1, 8192),
        jnp.transpose(master_weight, (1, 0, 2)),
        short_filter,
        medium_filter,
        medium_skip.reshape(1, 512),
        jnp.asarray(ftab),
        jnp.asarray(gtab),
    )
    return mixed[None], peak


def solution(mesh):
    placed = (
        P("dp", ("seq", "tensor"), None),
        P(),
        P(("dp", "seq"), None, "tensor"),
        P(None, None, "tensor"),
        P(None, "tensor"),
        P("tensor"),
    )
    return jax.shard_map(
        shards,
        mesh=mesh,
        in_specs=placed,
        out_specs=(P("dp", "seq", "tensor"), P()),
        check_vma=False,
    )
```

```python
import functools
import heapq

import jax
import jax.numpy as jnp
import numpy as np
from jax import lax
from jax.experimental import pallas as pl
from jax.experimental.pallas import tpu as pltpu
from jax.sharding import PartitionSpec as P

MESH = pl.DeviceIdType.MESH
F32 = jnp.float32
BF16 = jnp.bfloat16
eps_norm = 1e-06
eps_peak = 1e-06
grid_top = 448.0

ring_slots = [0, 1, -1, 2, -2, 3, -3, 4]
slot_of = {d: s for s, d in enumerate(ring_slots)}
slot_of[-4] = slot_of[4]

chunks = [(0, None), (-1, None), (1, None), (2, 0), (2, -1), (2, 1), (2, 2)]


def wrap4(d):
    return {-2: 2, 3: -1, -3: 1}.get(d, d)


def plan_messages():
    msgs = {}
    for ci, (dy, dx) in enumerate(chunks):
        size = 64 * 2 * (2048 if dx is None else 512)
        for sign, link in ((1, "zp"), (-1, "zm")):
            for hop in range(4):
                dep = [(link, ci, hop - 1)] if hop else []
                sub = None if hop < 3 else (0 if sign == 1 else 1)
                msgs[(link, ci, hop)] = (link, size if hop < 3 else size // 2, dep, ("tok", -sign * hop, sub, ci))
    quarter = 64 * 1536 * 2

    def ring(half, axis, fixed, need):
        first = 2 * half
        for sign in (1, -1):
            link = axis + ("p" if sign == 1 else "m")
            order = (first, first + 1) if sign == 1 else (first + 1, first)
            names = [(half, link, fixed, n) for n in range(3)]
            place = lambda d: (0, d) if axis == "x" else (d, 0)
            spot = lambda d: (fixed, d) if axis == "x" else (d, fixed)
            for n in range(2):
                msgs[names[n]] = (link, quarter, need(order[n]), ("w",) + spot(0) + (order[n],))
            msgs[names[2]] = (link, quarter, [names[0]], ("w",) + spot(-sign) + (order[0],))

    def arrival(half, axis, fixed, d, q):
        first = 2 * half
        if d == 0:
            return []
        if d == 2:
            return [(half, axis + ("p" if q == first else "m"), fixed, 2)]
        sign = -d
        order = (first, first + 1) if sign == 1 else (first + 1, first)
        return [(half, axis + ("p" if sign == 1 else "m"), fixed, order.index(q))]

    ring(0, "x", 0, lambda q: [])
    ring(1, "y", 0, lambda q: [])
    got = {}
    for d in (0, -1, 1, 2):
        for q in (0, 1):
            got[(0, d, q)] = arrival(0, "x", 0, d, q)
        for q in (2, 3):
            got[(d, 0, q)] = arrival(1, "y", 0, d, q)
    second = {}
    for d in (0, -1, 1, 2):
        tag0, tag1 = ("s", d), ("s", d)

        def ring2(half, axis, across):
            first = 2 * half
            for sign in (1, -1):
                link = axis + ("p" if sign == 1 else "m")
                order = (first, first + 1) if sign == 1 else (first + 1, first)
                names = [(half, link, ("s", across), n) for n in range(3)]
                spot = lambda e: (across, e) if axis == "x" else (e, across)
                for n in range(2):
                    key = spot(0) + (order[n],)
                    msgs[names[n]] = (link, quarter, got[key], ("w",) + spot(0) + (order[n],))
                msgs[names[2]] = (link, quarter, [names[0]], ("w",) + spot(-sign) + (order[0],))
            for e in (-1, 1, 2):
                for q in (first, first + 1):
                    if e == 2:
                        name = (half, axis + ("p" if q == first else "m"), ("s", across), 2)
                    else:
                        sign = -e
                        order = (first, first + 1) if sign == 1 else (first + 1, first)
                        name = (half, axis + ("p" if sign == 1 else "m"), ("s", across), order.index(q))
                    second[spot(e) + (q,)] = [name]

        ring2(0, "y", d)
        ring2(1, "x", d)
    got.update(second)
    for dy in (0, -1, 1, 2):
        for dx in (0, -1, 1, 2):
            for h in (0, 1):
                need = got[(dy, dx, 2 * h)] + got[(dy, dx, 2 * h + 1)]
                msgs[("pair", dy, dx, h)] = ("core", 2 * quarter, need, ("half", dy, dx, h))
    return msgs, got


def urgency(name):
    if name[0] in ("zp", "zm"):
        _, ci, hop = name
        at = (0.0, 4.0, 8.0, 12.0, 13.0, 14.0, 15.0)[ci]
        return at + 2.0 * hop if hop or ci > 2 else ci - 10.0
    if name[0] == "pair":
        return 0.0
    half, _, across, n = name
    if not isinstance(across, tuple):
        return n * 0.1
    d = {0: 0, -1: 1, 1: 2, 2: 3}[across[1]]
    if half == 0:
        return 10.0 + d * 0.1 + (10.0 if n == 2 else 0.0)
    return 10.0 + 4.0 * d + n * 0.1


def timeline(msgs):
    rate = {"z": 46.0e3, "x": 46.0e3, "y": 46.0e3, "c": 250.0e3}
    children = {}
    for name, (_, _, need, _) in msgs.items():
        for dep in need:
            children.setdefault(dep, []).append(name)
    rank = {name: i for i, name in enumerate(msgs)}
    left = {name: len(need) for name, (_, _, need, _) in msgs.items()}
    ready = {name: 0.0 for name in msgs}
    queue = {link: [] for link in ("zp", "zm", "xp", "xm", "yp", "ym", "core")}
    heap = []
    for name, (link, _, need, _) in msgs.items():
        if not need:
            ready[name] = 5.0 if link[0] == "z" else 15.0
            heapq.heappush(heap, (ready[name], 0, rank[name], name))
    busy = set()
    arrive, issue = {}, {}

    def serve(link, now):
        if link in busy or not queue[link]:
            return
        _, _, name = heapq.heappop(queue[link])
        busy.add(link)
        done = now + msgs[name][1] / rate[link[0]]
        arrive[name] = done + 1.5
        issue[name] = now
        heapq.heappush(heap, (done, 1, rank[name], name))
        for child in children.get(name, ()):
            left[child] -= 1
            ready[child] = max(ready[child], arrive[name])
            if left[child] == 0:
                heapq.heappush(heap, (ready[child], 0, rank[child], child))

    while heap:
        now, kind, _, name = heapq.heappop(heap)
        link = msgs[name][0]
        if kind == 1:
            busy.discard(link)
        else:
            heapq.heappush(queue[link], (urgency(name), rank[name], name))
        if not heap or heap[0][0] > now:
            for key in queue:
                serve(key, now)
    lead = 6.0
    early = {name: max(ready[name], issue[name] - lead) for name in msgs}
    return early, arrive


def plan():
    msgs, got = plan_messages()
    issue, arrive = timeline(msgs)
    tok_need = {}
    for ci, (dy, dx) in enumerate(chunks):
        tok_need[(dy, dx)] = [(link, ci, hop) for link in ("zp", "zm") for hop in range(4)]
    tasks = []
    for dy in (0, -1, 1, 2):
        for dx in (0, -1, 1, 2):
            need = list(tok_need[(dy, None)] if (dy, None) in tok_need else tok_need[(dy, dx)])
            for q in range(4):
                need += got[(dy, dx, q)]
            need += [("pair", dy, dx, h) for h in (0, 1)]
            tasks.append((max(arrive[n] for n in need), need, dy, dx))
    tasks.sort(key=lambda t: t[0])
    events = [(issue[name], 0, i, ("send", name)) for i, name in enumerate(msgs)]
    at = 0.0
    for i, (when, need, dy, dx) in enumerate(tasks):
        at = max(at, when + (3.0 if dy != 2 else 0.0))
        events.append((at, 1, i, ("dot", need, dy, dx)))
        at += 1.3
    events.sort(key=lambda e: e[:3])
    placed, order = set(), []
    for event in events:
        if event[3][0] == "send":
            assert all(dep in placed for dep in msgs[event[3][1]][2])
            placed.add(event[3][1])
        order.append(event[3])
    return msgs, order, at


def dft_tables():
    n = np.arange(256)
    k = np.arange(128)[:, None]
    angle = 2.0 * np.pi * ((k * n[None, :]) % 256) / 256.0
    lower = np.sin(angle)
    lower[0] = np.cos(np.pi * n)
    full = np.concatenate([np.cos(angle), lower], axis=0)

    def split(a):
        a = a.astype(np.float32)
        hi = a.astype(BF16)
        lo = (a - hi.astype(np.float32)).astype(BF16)
        return np.stack([hi, lo])

    return split(full), split(full[:, 128:].T)


def round_grid(v):
    m = jnp.abs(v)
    t = m * F32(8388609.0)
    top = t - t * F32(1.0 - 2.0**-24)
    quantum = jnp.maximum(top, F32(2.0**-6)) * F32(0.125)
    magic = quantum * F32(1.5 * 2.0**23)
    r = (m + magic) - magic
    r = jnp.where(m - r == quantum * F32(0.5), r + quantum, r)
    return jnp.where(v < 0, -r, r)


def kernel(
    program,
    tok_hbm, gain_hbm, w_hbm, sf_hbm, mf_hbm, skip_hbm, f_hbm, g_hbm,
    out_ref, peak_ref,
    tok_in, gain, w_in, sf, mf, skip, fmat, gmat,
    a_all, w_all, acc, feat, gext, hspec, peaks,
    local_sem, send_sem, recv_sem, pk_send, pk_recv, halo_send, halo_recv,
):
    msgs, events, ids = program
    y = lax.axis_index("dp")
    s = lax.axis_index("seq")
    z = lax.axis_index("tensor")
    x, c = s // 2, s % 2

    ins = [(w_hbm, w_in), (tok_hbm, tok_in), (gain_hbm, gain), (mf_hbm, mf), (f_hbm, fmat), (g_hbm, gmat), (sf_hbm, sf), (skip_hbm, skip)]
    loads = [pltpu.make_async_copy(src, dst, local_sem.at[i]) for i, (src, dst) in enumerate(ins)]
    for load in loads:
        load.start()

    def dev(dy, ds, dz):
        return ((y + dy) % 4, ds, (z + dz) % 8)

    barrier = pltpu.get_barrier_semaphore()
    peers = [dev(0, s, k) for k in range(1, 8)] + [dev(0, (s + k) % 8, 0) for k in range(1, 8)] + [dev(k, s, 0) for k in range(1, 4)]
    for peer in peers:
        pl.semaphore_signal(barrier, inc=1, device_id=peer, device_id_type=MESH)

    loads[0].wait()
    top = jnp.zeros((8, 512), F32)
    part = [jnp.zeros((8, 512), F32) for _ in range(4)]
    for k in range(3):
        for r in range(0, 256, 32):
            for j in range(4):
                part[j] = jnp.maximum(part[j], jnp.abs(w_in[k, r + 8 * j : r + 8 * j + 8, :]))
    top = jnp.maximum(jnp.maximum(part[0], part[1]), jnp.maximum(part[2], part[3]))
    top = jnp.max(jnp.max(top, axis=0, keepdims=True), axis=1, keepdims=True)
    peaks[0] = jnp.broadcast_to(top, (8, 128))

    def norm_rows(lo):
        for r in range(lo, lo + 32, 16):
            v = tok_in[r : r + 16, :].astype(F32)
            mean = jnp.sum(v * v, axis=1, keepdims=True) * F32(1.0 / 8192)
            a_all[r : r + 16, :] = (v * lax.rsqrt(mean + F32(eps_norm)) * gain[...]).astype(BF16)

    loads[1].wait()
    loads[2].wait()
    norm_rows(0)
    norm_rows(32)

    def peak_round(src, base, targets):
        copies = []
        for i, target in enumerate(targets):
            copies.append(
                pltpu.make_async_remote_copy(
                    src_ref=peaks.at[src], dst_ref=peaks.at[3 + base + i],
                    send_sem=pk_send.at[base + i], recv_sem=pk_recv.at[base + i],
                    device_id=target, device_id_type=MESH,
                )
            )
        for copy in copies:
            copy.start()
        return copies

    def peak_finish(copies, src, base):
        best = peaks[src]
        for i, copy in enumerate(copies):
            copy.wait_recv()
            best = jnp.maximum(best, peaks[3 + base + i])
        return best

    def w_row(dy, dx, parity):
        return (((y + dy) % 4) * 8 + ((x + dx) % 4) * 2 + parity) * 256

    def message(name):
        link, _, _, place = msgs[name]
        if place[0] == "tok":
            _, d, sub, ci = place
            step = 1 if link == "zp" else -1
            off, rows = (0, 64) if sub is None else (32 * sub, 32)
            here = slot_of[d] * 64 + off
            there = slot_of[d - step] * 64 + off
            dy, dx = chunks[ci]
            if dx is None:
                cols = pl.ds(pl.multiple_of(((y + dy) % 4) * 2048, 2048), 2048)
            else:
                cols = pl.ds(pl.multiple_of(w_row(dy, dx, 0), 512), 512)
            src, dst = a_all.at[here : here + rows, cols], a_all.at[there : there + rows, cols]
            target = dev(0, s, step)
        elif place[0] == "w":
            _, dy, dx, q = place
            row = pl.multiple_of(w_row(dy, dx, c) + 64 * q, 64)
            src = dst = w_all.at[pl.ds(row, 64), :]
            if link[0] == "x":
                target = dev(0, (s + (2 if link[1] == "p" else 6)) % 8, 0)
            else:
                target = dev(1 if link[1] == "p" else 3, s, 0)
        else:
            _, dy, dx, h = place
            row = pl.multiple_of(w_row(dy, dx, c) + 128 * h, 128)
            src = dst = w_all.at[pl.ds(row, 128), :]
            target = (y, x * 2 + 1 - c, z)
        i = ids[name]
        return pltpu.make_async_remote_copy(
            src_ref=src, dst_ref=dst, send_sem=send_sem.at[i], recv_sem=recv_sem.at[i], device_id=target, device_id_type=MESH
        )

    copies = {name: message(name) for name in msgs}
    arrived = set()
    started = [(link, ci, 0) for ci in range(3) for link in ("zp", "zm")]

    def need(names):
        for name in names:
            if name not in arrived:
                arrived.add(name)
                copies[name].wait_recv()

    pl.semaphore_wait(barrier, len(peers))
    round0 = peak_round(0, 0, peers[:7])
    for name in started:
        copies[name].start()
    peaks[1] = peak_finish(round0, 0, 0)
    round1 = peak_round(1, 7, peers[7:14])
    peaks[2] = peak_finish(round1, 1, 7)
    round2 = peak_round(2, 14, peers[14:])
    peak = peak_finish(round2, 2, 14)
    peak_ref[0] = jnp.max(peak)

    ratio = F32(grid_top) / (peak + F32(eps_peak))
    factor = jnp.ones((8, 128), F32)
    inverse = jnp.ones((8, 128), F32)
    for p in (16, 8, 4, 2, 1):
        larger = factor * F32(2.0**p)
        over = ratio >= larger
        factor = jnp.where(over, larger, factor)
        inverse = jnp.where(over, inverse * F32(2.0**-p), inverse)
    factor = jnp.broadcast_to(factor[0:1, 0:1], (1, 512))
    inverse = jnp.broadcast_to(inverse[0:1, 0:1], (1, 512))
    own = pl.multiple_of(w_row(0, 0, c), 256)

    def recast(i, carry):
        r = pl.multiple_of(i * 32, 32)
        for k in range(3):
            w_all[pl.ds(own + r, 32), 512 * k : 512 * k + 512] = round_grid(w_in[k, pl.ds(r, 32), :] * factor).astype(BF16)
        return carry

    lax.fori_loop(0, 8, recast, 0)

    def spectrum():
        for load in loads[3:]:
            load.wait()
        taps = mf[...]
        h = jnp.dot(fmat[0, :, 0:128], taps, preferred_element_type=F32) + jnp.dot(fmat[1, :, 0:128], taps, preferred_element_type=F32)
        first = lax.broadcasted_iota(jnp.int32, (128, 512), 0) == 0
        scale = jnp.where(first, F32(1.0 / 256), F32(2.0 / 256))
        hc, hs = h[0:128] * scale, h[128:256] * scale
        hspec[0] = hc
        hspec[1] = jnp.where(first, F32(0.0), hs)
        hspec[2] = jnp.where(first, hs, hc)

    def product(dy, dx, fresh):
        k0 = pl.multiple_of(w_row(dy, dx, 0), 512)

        def column(i, carry):
            n = pl.multiple_of(i * 512, 512)
            got = jnp.dot(a_all[:, pl.ds(k0, 512)], w_all[pl.ds(k0, 512), pl.ds(n, 512)], preferred_element_type=F32)
            if fresh:
                acc[:, pl.ds(n, 512)] = got
            else:
                acc[:, pl.ds(n, 512)] += got
            return carry

        lax.fori_loop(0, 3, column, 0)

    fresh = True
    ready = False
    for event in events:
        if event[0] == "send":
            name = event[1]
            if name in started:
                continue
            need(msgs[name][2])
            copies[name].start()
            if not ready and msgs[name][2]:
                ready = True
                spectrum()
        else:
            _, names, dy, dx = event
            need(names)
            product(dy, dx, fresh)
            fresh = False

    inverse_row = inverse
    for slot, d in enumerate(ring_slots):
        row = pl.multiple_of(8 + 64 * ((z + d) % 8), 8)
        for k in range(3):
            cols = slice(512 * k, 512 * k + 512)
            feat[pl.ds(row, 64), cols] = (acc[64 * slot : 64 * slot + 64, cols] * inverse_row).astype(BF16).astype(F32)

    after = (y, (s + 1) % 8, z)
    rim = pltpu.make_async_remote_copy(
        src_ref=feat.at[512:520, :], dst_ref=feat.at[0:8, :], send_sem=halo_send.at[0], recv_sem=halo_recv.at[0],
        device_id=after, device_id_type=MESH,
    )
    rim.start()

    def short(k, lo, rows):
        total = jnp.zeros((rows, 512), F32)
        for j in range(3):
            total = total + sf[k, j : j + 1, :] * feat[8 + lo - j : 8 + lo - j + rows, 512 * k : 512 * k + 512]
        return total

    def gate(lo, rows):
        gext[128 + lo : 128 + lo + rows, :] = (short(1, lo, rows) * short(2, lo, rows)).astype(BF16)

    gate(384, 128)
    edge = pltpu.make_async_remote_copy(
        src_ref=gext.at[512:640, :], dst_ref=gext.at[0:128, :], send_sem=halo_send.at[1], recv_sem=halo_recv.at[1],
        device_id=after, device_id_type=MESH,
    )
    edge.start()
    gate(256, 128)
    gate(128, 128)
    gate(16, 112)

    def mix(b):
        lo = 128 * b
        e = gext[lo : lo + 256, :]
        t = jnp.dot(fmat[0], e, preferred_element_type=F32) + jnp.dot(fmat[1], e, preferred_element_type=F32)
        tc, ts = t[0:128], t[128:256]
        pc = tc * hspec[0] - ts * hspec[1]
        ps = tc * hspec[1] + ts * hspec[2]
        p = jnp.concatenate([pc, ps], axis=0)
        ph = p.astype(BF16)
        pl_ = (p - ph.astype(F32)).astype(BF16)
        f = jnp.dot(gmat[0], ph, preferred_element_type=F32)
        f = f + jnp.dot(gmat[0], pl_, preferred_element_type=F32)
        f = f + jnp.dot(gmat[1], ph, preferred_element_type=F32)
        f = f + skip[...] * e[128:256].astype(F32)
        out_ref[lo : lo + 128, :] = (short(0, lo, 128) * f).astype(BF16)

    mix(3)
    mix(2)
    rim.wait_recv()
    edge.wait_recv()

    @pl.when(s == 0)
    def _():
        feat[0:8, :] = jnp.zeros((8, 1536), F32)
        gext[0:128, :] = jnp.zeros((128, 512), BF16)

    gate(0, 16)
    mix(1)
    mix(0)
    rim.wait_send()
    edge.wait_send()
    for copy in round0 + round1 + round2:
        copy.wait_send()
    for copy in copies.values():
        copy.wait_send()


def shards(tokens, norm_gain, master_weight, short_filter, medium_filter, medium_skip):
    msgs, events, _ = plan()
    ids = {name: i for i, name in enumerate(msgs)}
    ftab, gtab = dft_tables()
    count = len(msgs)
    any_space = pl.BlockSpec(memory_space=pl.ANY)
    mixed, peak = pl.pallas_call(
        functools.partial(kernel, (msgs, events, ids)),
        out_shape=(jax.ShapeDtypeStruct((512, 512), BF16), jax.ShapeDtypeStruct((1,), F32)),
        in_specs=[any_space] * 8,
        out_specs=(pl.BlockSpec(memory_space=pltpu.VMEM), pl.BlockSpec(memory_space=pltpu.SMEM)),
        scratch_shapes=[
            pltpu.VMEM((64, 8192), BF16),
            pltpu.VMEM((1, 8192), F32),
            pltpu.VMEM((3, 256, 512), F32),
            pltpu.VMEM((3, 3, 512), F32),
            pltpu.VMEM((128, 512), BF16),
            pltpu.VMEM((1, 512), F32),
            pltpu.VMEM((2, 256, 256), BF16),
            pltpu.VMEM((2, 128, 256), BF16),
            pltpu.VMEM((512, 8192), BF16),
            pltpu.VMEM((8192, 1536), BF16),
            pltpu.VMEM((512, 1536), F32),
            pltpu.VMEM((520, 1536), F32),
            pltpu.VMEM((640, 512), BF16),
            pltpu.VMEM((3, 128, 512), F32),
            pltpu.VMEM((20, 8, 128), F32),
            pltpu.SemaphoreType.DMA((8,)),
            pltpu.SemaphoreType.DMA((count,)),
            pltpu.SemaphoreType.DMA((count,)),
            pltpu.SemaphoreType.DMA((17,)),
            pltpu.SemaphoreType.DMA((17,)),
            pltpu.SemaphoreType.DMA((2,)),
            pltpu.SemaphoreType.DMA((2,)),
        ],
        compiler_params=pltpu.CompilerParams(collective_id=0, has_side_effects=True, vmem_limit_bytes=60 * 1024 * 1024),
    )(
        tokens.reshape(64, 8192),
        norm_gain.reshape(1, 8192),
        jnp.transpose(master_weight, (1, 0, 2)),
        short_filter,
        medium_filter,
        medium_skip.reshape(1, 512),
        jnp.asarray(ftab),
        jnp.asarray(gtab),
    )
    return mixed[None], peak


def solution(mesh):
    placed = (
        P("dp", ("seq", "tensor"), None),
        P(),
        P(("dp", "seq"), None, "tensor"),
        P(None, None, "tensor"),
        P(None, "tensor"),
        P("tensor"),
    )
    return jax.shard_map(
        shards,
        mesh=mesh,
        in_specs=placed,
        out_specs=(P("dp", "seq", "tensor"), P()),
        check_vma=False,
    )
```
